256 devices in a mesh: occ: 8 (over z_hi, core), aux: 32 (over x, z_lo, y).
Axes of the slice: x: 4, y: 4, z: 8 (z_hi: 4, z_lo: 2; z = z_hi * 2 + z_lo), core: 2. Of those that a mesh axis runs over, the one named last changes fastest.
Arguments:
- coeffs: bfloat16 [8, 256, 131072], P('occ', None, 'aux'), may hold values from -0.31445312 to 0.31445312
- occ_energy: bfloat16 [8], P('occ'), may hold values from -1.5 to -0.29882812
- virt_energy: bfloat16 [256], replicated, may hold values from 0.19921875 to 3
- screen: int32 [8, 1024], P('occ', 'aux'), may hold values 0 or 1
- owner: int32 [1024], P('aux'), may hold values from 0 to 127
- positions: float32 [3, 128], replicated, may hold values from -1 to 1
Outputs:
- gamma: bfloat16 [8, 256, 131072], P('occ', None, 'aux')
- virial: float32 [9, 131072], P(None, 'aux')
The draws below stay inside these ranges and needn't reach their ends.
All inputs are finite; a program needn't handle non-finite values. No bound on the sum of `screen` on one device may be relied on, other than what follows from the above.
Results may differ from the reference program's by a relative error of at most 0.0049.
Values may be sent and summed in bfloat16 or wider, within the bound.
A program may use at most 64 MiB of HBM per device.

```python
import jax
import jax.numpy as jnp
from jax import lax

OCC_DEV = 1
VIRT = 256
ABLK = 128
ATOMS = 128
NOCC = 8
NAUX = 131072
ABLOCKS = 1024
N_OCC = 8


def with_ends(entries, stream_key, smallest, largest):
    longest = entries.shape.index(max(entries.shape))
    spots = []
    for shift in (0, 1):
        where = [jax.random.randint(jax.random.fold_in(stream_key, axis), (), 0, length) for axis, length in enumerate(entries.shape)]
        where[longest] = (where[longest] + shift) % entries.shape[longest]
        spots.append(tuple(where))
    return entries.at[spots[0]].set(smallest).at[spots[1]].set(largest)


def block_scale(stream_key, shape, pieces, least, top_value):
    loudness = 1.0
    for position, parts in pieces:
        heights = jax.random.uniform(jax.random.fold_in(jax.random.fold_in(stream_key, 6), position), (parts,), jnp.float32, least / len(pieces), top_value / len(pieces))
        loudness = loudness * jnp.repeat(jnp.exp(heights), shape[position] // parts).reshape((-1,) + (1,) * (len(shape) - 1 - position))
    return loudness


def bell_draw(stream_key, shape, width, most, pieces=(), kind=jnp.bfloat16):
    loudness = block_scale(stream_key, shape, pieces, -0.22, 0.18) if pieces else 1.0
    array = jax.random.normal(stream_key, shape, jnp.float32) * width * loudness
    return jnp.minimum(jnp.maximum(array, -most), most).astype(kind)


def setup_inputs(seed: int = 0) -> dict:
    arg_keys = jax.random.split(jax.random.key(seed), 7)
    return {
        "coeffs": bell_draw(arg_keys[0], (NOCC, VIRT, NAUX), (NAUX ** -0.25), 0.31445312, ((0, 8), (2, 32))),
        "occ_energy": jnp.clip(-1.5 + 1.2011719 * jax.random.uniform(arg_keys[1], (NOCC,), jnp.float32) ** block_scale(arg_keys[1], (NOCC,), ((0, 8),), -0.2, 0.2), -1.5, -0.29882812).astype(jnp.bfloat16),
        "virt_energy": jnp.clip(jax.random.uniform(arg_keys[2], (VIRT,), jnp.float32, 0.19921875, 3.0), 0.19921875, 3.0).astype(jnp.bfloat16),
        "screen": with_ends((jax.random.randint(arg_keys[3], (N_OCC, ABLOCKS), 0, 3) < 2).astype(jnp.int32), jax.random.fold_in(arg_keys[3], 1), 0, 1),
        "owner": with_ends(jax.random.randint(arg_keys[4], (ABLOCKS,), 0, ATOMS), jax.random.fold_in(arg_keys[4], 1), 0, ATOMS - 1).astype(jnp.int32),
        "positions": jnp.clip(jax.random.uniform(arg_keys[5], (3, ATOMS), jnp.float32, -1.0, 1.0), -1.0, 1.0),
    }


def reference(coeffs, occ_energy, virt_energy, screen, owner, positions):
    mask = jnp.repeat(jnp.repeat(screen, OCC_DEV, axis=0), ABLK, axis=1).astype(jnp.bfloat16)
    masked = coeffs * mask[:, None, :]
    flat = masked.reshape(NOCC * VIRT, NAUX).astype(jnp.float32)
    pairs = jnp.dot(flat, flat.T, precision=lax.Precision.HIGHEST)
    spread = (virt_energy.astype(jnp.float32)[None, :] - occ_energy.astype(jnp.float32)[:, None]).reshape(-1)
    amps = (pairs / (spread[:, None] + spread[None, :])).astype(jnp.bfloat16)
    gamma = jnp.dot(amps.astype(jnp.float32), flat, precision=lax.Precision.HIGHEST).astype(jnp.bfloat16)
    weight = jnp.sum(gamma.astype(jnp.float32) * flat, axis=0)
    where = jnp.repeat(positions[:, owner], ABLK, axis=1)
    virial = (where[:, None, :] * where[None, :, :]).reshape(9, NAUX) * weight[None, :]
    return gamma.reshape(NOCC, VIRT, NAUX), virial
```

```python
import functools

import jax
import jax.numpy as jnp
from jax import lax
from jax.experimental import pallas as pl
from jax.experimental.pallas import tpu as pltpu
from jax.sharding import PartitionSpec as P

MESH = pl.DeviceIdType.MESH
F32, BF16 = jnp.float32, jnp.bfloat16

ABLK = 128
VIRT = 256
COLS = 512
TAIL = 16
CHUNK = 16
NBLK = 10
EARLY = 6

SLOTS = ((0, 0), (1, 1), (3, 3), (0, 1), (3, 0), (1, 3), (2, 2), (1, 2), (2, 3), (0, 2))
GROUPS = ((0, EARLY), (EARLY, NBLK))


def dot_nt(a, b):
    return lax.dot_general(a, b, (((1,), (1,)), ((), ())), preferred_element_type=F32)


def dot_nn(a, b):
    return lax.dot_general(a, b, (((1,), (0,)), ((), ())), preferred_element_type=F32)


def dot_tn(a, b):
    return lax.dot_general(a, b, (((0,), (0,)), ((), ())), preferred_element_type=F32)


def kernel(
    coeffs, mask, energy, vrow, vcol, owner, atoms,
    gamma, virial,
    slabs, rows, part, plane_in, plane_sum, z_in, z_amps, amps, turned, gout, wmine, wall, where,
    sa, ra, sf, rf, sp, rp, sz, rz, sy, ry, sg, rg, sh, rh, sb, rb, sw, rw,
):
    o = lax.axis_index("occ")
    a = lax.axis_index("aux")
    c, h = o // 2, o % 2
    y, zl, x = a % 4, (a // 4) % 2, a // 8
    z = c * 2 + zl
    q = x * 4 + y
    other = 1 - h

    def at(x_, y_, z_, h_):
        return {"occ": (z_ // 2) * 2 + h_, "aux": (x_ * 2 + z_ % 2) * 4 + y_}

    partner = at(x, y, z, other)
    occ_peers = {}
    for dc in (1, 3, 2):
        for dh in (0, 1):
            occ_peers[dc, dh] = at(x, y, (z + 2 * dc) % 8, (h + dh) % 2)
    plane_peers = {}
    for dx in range(4):
        for dy in range(4):
            if (dx, dy) != (0, 0):
                plane_peers[dx * 4 + dy] = (
                    at((x + dx) % 4, (y + dy) % 4, z, h),
                    ((x + dx) % 4) * 4 + (y + dy) % 4,
                )
    z_peers = {dz: (at(x, y, (z + dz) % 8, h), (z + dz) % 8) for dz in range(1, 8)}

    barrier = pltpu.get_barrier_semaphore()
    greet = [partner, *occ_peers.values()]
    greet += [d for d, _ in plane_peers.values()]
    greet += [d for dz, (d, _) in z_peers.items() if dz % 2]
    for d in greet:
        pl.semaphore_signal(barrier, inc=1, device_id=d, device_id_type=MESH)

    sent = []

    def send(src, dst, ss, rs, d):
        cp = pltpu.make_async_remote_copy(
            src_ref=src, dst_ref=dst, send_sem=ss, recv_sem=rs, device_id=d, device_id_type=MESH
        )
        cp.start()
        sent.append(cp)
        return cp

    def mask_slab(k, _):
        cols = pl.ds(pl.multiple_of(k * COLS, COLS), COLS)
        slabs[k, 0:VIRT, :] = coeffs[:, cols] * mask[:, cols]
        slabs[k, VIRT:, :] = energy[...]
        return 0

    lax.fori_loop(0, 8, mask_slab, 0)

    def keep_slab(half, _):
        rows[o, half] = slabs[c * 2 + half]
        return 0

    lax.fori_loop(0, 2, keep_slab, 0)

    pl.semaphore_wait(barrier, len(greet))

    to_partner = send(rows.at[o], rows.at[o], sa.at[6], ra.at[6], partner)
    slab_in = {}
    for n, (key, d) in enumerate(occ_peers.items()):
        dc, dh = key
        dst_o = ((c + dc) % 4) * 2 + (h + dh) % 2
        slab_in[key] = send(slabs.at[dst_o], rows.at[o, (h + dh) % 2], sa.at[n], ra.at[n], d)

    def place(k, _):
        cols = pl.ds(pl.multiple_of(k * COLS, COLS), COLS)
        ids = lax.broadcasted_iota(jnp.int32, (128, COLS), 0)
        onehot = (ids == owner[:, cols]).astype(F32)
        where[:, cols] = lax.dot_general(
            atoms[...], onehot, (((1,), (0,)), ((), ())),
            precision=lax.Precision.HIGHEST, preferred_element_type=F32,
        )
        return 0

    lax.fori_loop(0, 8, place, 0)

    def product(slot):
        r0, r1 = SLOTS[slot]
        first, second = (c + r0) % 4, (c + r1) % 4
        if slot in (5, 9):
            first, second = jnp.minimum(first, second), jnp.maximum(first, second)
        lead = first * 2 + h

        def column(hc, _):
            co = second * 2 + hc
            s = dot_nt(rows[lead, 0, 0:VIRT], rows[co, 0, 0:VIRT])
            s += dot_nt(rows[lead, 1, 0:VIRT], rows[co, 1, 0:VIRT])
            part[slot, :, pl.ds(pl.multiple_of(hc * VIRT, VIRT), VIRT)] = s.astype(BF16)
            return 0

        lax.fori_loop(0, 2, column, 0)

    def pass_on(keys):
        out = []
        for key in keys:
            dc, dh = key
            n = list(occ_peers).index(key)
            slab_in[key].wait_recv()
            src_o = ((c + 4 - dc) % 4) * 2 + (h + dh) % 2
            out.append(send(rows.at[src_o, h], rows.at[src_o, h], sf.at[n], rf.at[n], partner))
        for cp in out:
            cp.wait_recv()

    plane_wait = {}

    def share_products(g):
        lo, hi = GROUPS[g]
        for j, (d, qd) in plane_peers.items():
            there = pl.ds(pl.multiple_of(qd * CHUNK, CHUNK), CHUNK)
            plane_wait[g, j] = send(
                part.at[lo:hi, there, :], plane_in.at[j, lo:hi], sp.at[g, j], rp.at[g, j], d
            )

    mine = pl.ds(pl.multiple_of(q * CHUNK, CHUNK), CHUNK)

    def block_id(slot):
        r0, r1 = SLOTS[slot]
        if r0 == r1:
            return (c + r0) % 4
        if slot in (5, 9):
            return 8 + (c + r0) % 2
        return 4 + (c + r0) % 4

    def sum_plane(g):
        lo, hi = GROUPS[g]
        for j in plane_peers:
            plane_wait[g, j].wait_recv()
        for slot in range(lo, hi):
            s = part[slot, mine, :].astype(F32)
            for j in plane_peers:
                s += plane_in[j, slot].astype(F32)
            plane_sum[block_id(slot)] = s

    to_partner.wait_recv()
    product(0)
    pass_on([(1, 0), (1, 1), (3, 0), (3, 1)])
    for slot in range(1, EARLY):
        product(slot)
    share_products(0)
    pass_on([(2, 0), (2, 1)])
    for slot in range(EARLY, NBLK):
        product(slot)
    share_products(1)
    sum_plane(0)
    sum_plane(1)

    def share_of(k):
        return (
            pl.ds((k // 4) * 5, 5),
            slice(None),
            pl.ds(pl.multiple_of((k % 4) * 128, 128), 128),
        )

    z_wait = {}
    for dz, (d, zd) in z_peers.items():
        z_wait[dz] = send(plane_sum.at[share_of(zd)], z_in.at[dz], sz.at[dz], rz.at[dz], d)
    for dz in z_peers:
        z_wait[dz].wait_recv()

    hc = (z % 4) // 2
    va = vrow[mine, :]
    vb = vcol[:, pl.ds(pl.multiple_of((z % 2) * 128, 128), 128)]
    lanes = pl.ds(pl.multiple_of((z % 4) * 128, 128), 128)
    for t in range(5):
        b = (z // 4) * 5 + t
        s = plane_sum[b, :, lanes]
        for dz in z_peers:
            s += z_in[dz, t]
        near = b % 4
        lead = near * 2 + h
        far = jnp.where(b < 4, near, jnp.where(b < 8, (near + 1) % 4, near + 2))
        ea = rows[lead, h, VIRT:, 0:128].astype(F32)
        eb = rows[far * 2 + hc, h, VIRT:, 0:128].astype(F32)
        z_amps[b, :, lanes] = (s / ((va - ea) + (vb - eb))).astype(BF16)
    y_wait = {}
    for dz, (d, _) in z_peers.items():
        y_wait[dz] = send(
            z_amps.at[share_of(z)], z_amps.at[share_of(z)], sy.at[dz], ry.at[dz], d
        )
    for dz in z_peers:
        y_wait[dz].wait_recv()

    here = pl.ds(pl.multiple_of(h * VIRT + q * CHUNK, CHUNK), CHUNK)
    for slot in range(NBLK):
        amps[slot, here, :] = z_amps[block_id(slot)]
    g_wait = {}
    for g in (1, 0):
        lo, hi = GROUPS[g]
        piece = amps.at[lo:hi, here, :]
        g_wait[g, 0] = send(piece, piece, sh.at[g, 0], rh.at[g, 0], partner)
        for j, (d, _) in plane_peers.items():
            g_wait[g, j] = send(piece, piece, sg.at[g, j], rg.at[g, j], d)

    def collect(g):
        lo, hi = GROUPS[g]
        out = [g_wait[g, 0]]
        for j in plane_peers:
            dx, dy = j // 4, j % 4
            src_q = ((x + 4 - dx) % 4) * 4 + (y + 4 - dy) % 4
            g_wait[g, j].wait_recv()
            piece = amps.at[lo:hi, pl.ds(pl.multiple_of(h * VIRT + src_q * CHUNK, CHUNK), CHUNK), :]
            out.append(send(piece, piece, sh.at[g, j], rh.at[g, j], partner))
        for cp in out:
            cp.wait_recv()
        n = 1 - g
        slot, low = ((9, c < 2), (5, (c + 1) % 4 < 2))[n]

        @pl.when(low)
        def _():
            turned[n] = amps[slot]

        @pl.when(jnp.logical_not(low))
        def _():
            turned[n] = amps[slot].T

    def factor(r, rc, hr):
        span = pl.ds(pl.multiple_of(hr * VIRT, VIRT), VIRT)
        for slot, pair in enumerate(SLOTS):
            ref = turned.at[0] if slot == 9 else turned.at[1] if slot == 5 else amps.at[slot]
            if pair == (r, rc):
                return dot_nn, ref, (span, None)
            if pair == (rc, r):
                return dot_tn, ref, (None, span)
        raise AssertionError

    weight = jnp.zeros((1, COLS), F32)
    b_wait = {}

    def gamma_rows(r, dh, weight):
        hr = (h + dh) % 2
        ro = ((c + r) % 4) * 2 + hr
        acc = None
        for rc in range(4):
            dot, ref, (rs, cs) = factor(r, rc, hr)
            for hcol in range(2):
                half = slice(hcol * VIRT, (hcol + 1) * VIRT)
                block = ref[rs, half] if cs is None else ref[half, cs]
                term = dot(block, rows[((c + rc) % 4) * 2 + hcol, h, 0:VIRT])
                acc = term if acc is None else acc + term
        out = acc.astype(BF16)
        weight += jnp.sum(out.astype(F32) * rows[ro, h, 0:VIRT].astype(F32), axis=0, keepdims=True)
        cols = pl.ds(pl.multiple_of(o * COLS, COLS), COLS)
        if (r, dh) == (0, 0):
            gamma[:, cols] = out
        else:
            gout[ro] = out
            d = partner if r == 0 else occ_peers[r, dh]
            n = r * 2 + dh
            b_wait[n] = send(gout.at[ro], gamma.at[:, cols], sb.at[n], rb.at[n], d)
        return weight

    collect(1)
    for dh in (0, 1):
        weight = gamma_rows(2, dh, weight)
    collect(0)
    for r in (1, 3, 0):
        for dh in (1, 0):
            weight = gamma_rows(r, dh, weight)

    wmine[...] = jnp.broadcast_to(weight, (8, COLS))
    wall[o] = jnp.broadcast_to(weight, (8, COLS))
    w_wait = [send(wmine, wall.at[o], sw.at[6], rw.at[6], partner)]
    for n, d in enumerate(occ_peers.values()):
        w_wait.append(send(wmine, wall.at[o], sw.at[n], rw.at[n], d))
    for cp in w_wait:
        cp.wait_recv()

    def terms(k, _):
        cols = pl.ds(pl.multiple_of(k * COLS, COLS), COLS)
        w = wall[k, 0:1, :]
        for i in range(3):
            for j in range(3):
                virial[3 * i + j : 3 * i + j + 1, cols] = where[i : i + 1, cols] * where[j : j + 1, cols] * w
        return 0

    lax.fori_loop(0, 8, terms, 0)
    for cp in b_wait.values():
        cp.wait_recv()
    for cp in sent:
        cp.wait_send()


def body(coeffs, occ_energy, virt_energy, screen, owner, positions):
    occ_dev, virt, aux_dev = coeffs.shape
    mask = jnp.repeat(screen, ABLK, axis=1).astype(BF16)
    owners = jnp.repeat(owner[None, :], ABLK, axis=1)
    energy = jnp.broadcast_to(occ_energy[:, None], (TAIL, COLS))
    virt_f = virt_energy.astype(F32)
    vrow = jnp.broadcast_to(virt_f[:, None], (VIRT, 128))
    vcol = jnp.broadcast_to(virt_f[None, :], (CHUNK, VIRT))
    atoms = jnp.pad(positions, ((0, 5), (0, 0)))
    vmem = pl.BlockSpec(memory_space=pltpu.VMEM)
    dma = pltpu.SemaphoreType.DMA
    gamma, virial = pl.pallas_call(
        kernel,
        out_shape=(
            jax.ShapeDtypeStruct((VIRT, aux_dev), BF16),
            jax.ShapeDtypeStruct((9, aux_dev), F32),
        ),
        in_specs=[vmem] * 7,
        out_specs=(vmem, vmem),
        scratch_shapes=[
            pltpu.VMEM((8, VIRT + TAIL, COLS), BF16),
            pltpu.VMEM((8, 2, VIRT + TAIL, COLS), BF16),
            pltpu.VMEM((NBLK, VIRT, 2 * VIRT), BF16),
            pltpu.VMEM((16, NBLK, CHUNK, 2 * VIRT), BF16),
            pltpu.VMEM((NBLK, CHUNK, 2 * VIRT), F32),
            pltpu.VMEM((8, 5, CHUNK, 128), F32),
            pltpu.VMEM((NBLK, CHUNK, 2 * VIRT), BF16),
            pltpu.VMEM((NBLK, 2 * VIRT, 2 * VIRT), BF16),
            pltpu.VMEM((2, 2 * VIRT, 2 * VIRT), BF16),
            pltpu.VMEM((8, VIRT, COLS), BF16),
            pltpu.VMEM((8, COLS), F32),
            pltpu.VMEM((8, 8, COLS), F32),
            pltpu.VMEM((8, aux_dev), F32),
            dma((7,)), dma((7,)), dma((6,)), dma((6,)),
            dma((2, 16)), dma((2, 16)), dma((8,)), dma((8,)), dma((8,)), dma((8,)),
            dma((2, 16)), dma((2, 16)), dma((2, 16)), dma((2, 16)),
            dma((8,)), dma((8,)), dma((7,)), dma((7,)),
        ],
        compiler_params=pltpu.CompilerParams(
            collective_id=0, has_side_effects=True, vmem_limit_bytes=60 * 1024 * 1024
        ),
    )(coeffs.reshape(VIRT, aux_dev), mask, energy, vrow, vcol, owners, atoms)
    return gamma.reshape(occ_dev, virt, aux_dev), virial


def solution(mesh):
    placed = (P("occ", None, "aux"), P("occ"), P(), P("occ", "aux"), P("aux"), P())
    return jax.shard_map(
        body,
        mesh=mesh,
        in_specs=placed,
        out_specs=(P("occ", None, "aux"), P(None, "aux")),
        check_vma=False,
    )
```

```python
import jax
import jax.numpy as jnp
from jax import lax
from jax.experimental import pallas as pl
from jax.experimental.pallas import tpu as pltpu
from jax.sharding import PartitionSpec as P

MESH = pl.DeviceIdType.MESH
F32, BF16 = jnp.float32, jnp.bfloat16

ABLK = 128
VIRT = 256
COLS = 512
TAIL = 16
CHUNK = 16
NBLK = 10
EARLY = 6

SLOTS = ((0, 0), (1, 1), (3, 3), (0, 1), (3, 0), (1, 3), (1, 2), (2, 3), (0, 2), (2, 2))
OPEN = (5, 8)
GROUPS = ((0, EARLY), (EARLY, NBLK))
SPREADS = ((1, 8), (8, 9), (0, 1))


def dot_nt(a, b):
    return lax.dot_general(a, b, (((1,), (1,)), ((), ())), preferred_element_type=F32)


def dot_nn(a, b):
    return lax.dot_general(a, b, (((1,), (0,)), ((), ())), preferred_element_type=F32)


def dot_tn(a, b):
    return lax.dot_general(a, b, (((0,), (0,)), ((), ())), preferred_element_type=F32)


def kernel(
    screen, owner, coeffs, energies, positions,
    gamma, virial,
    raw, slabs, rows, also, vrow, part, plane_in, plane_sum, z_in, z_amps, amps, turned, gout,
    wmine, wall, where,
    sl, sa, ra, sr, rr, st, rt, sf, rf, sm, rm, sp, rp, sz, rz, sy, ry, sg, rg, sh, rh, sb, rb, sw, rw,
):
    o = lax.axis_index("occ")
    a = lax.axis_index("aux")
    c, h = o // 2, o % 2
    y, zl, x = a % 4, (a // 4) % 2, a // 8
    z = c * 2 + zl
    q = x * 4 + y
    other = 1 - h
    side = 1 - 2 * h

    def chip(n):
        return (c + n + 8) % 4

    def at(x_, y_, z_, h_):
        return {"occ": (z_ // 2) * 2 + h_, "aux": (x_ * 2 + z_ % 2) * 4 + y_}

    partner = at(x, y, z, other)
    def on_ring(chip_, h_):
        return at(x, y, chip_ * 2 + zl, h_)

    buddy = on_ring(chip(-side), other)
    buddy_o = chip(-side) * 2 + other
    near = {}
    far = {}
    for flip in (0, 1):
        there = (h + flip) % 2
        for way in (0, 1):
            to = chip(side if way == 0 else -side)
            near[way, flip] = (on_ring(to, there), to * 2 + there)
        far[flip] = (on_ring(chip(2 * there - 1), there), chip(2) * 2 + 1 - there)
    plane_peers = {}
    for dx in range(4):
        for dy in range(4):
            if (dx, dy) != (0, 0):
                plane_peers[dx * 4 + dy] = (
                    at((x + dx) % 4, (y + dy) % 4, z, h),
                    ((x + dx) % 4) * 4 + (y + dy) % 4,
                )
    z_peers = {dz: (at(x, y, (z + dz) % 8, h), (z + dz) % 8) for dz in range(1, 8)}

    barrier = pltpu.get_barrier_semaphore()
    everyone = [partner, *(d for d, _ in near.values()), on_ring(chip(2), h), on_ring(chip(2), other)]
    greet = [*everyone]
    greet += [d for d, _ in plane_peers.values()]
    greet += [d for dz, (d, _) in z_peers.items() if dz % 2]
    for d in greet:
        pl.semaphore_signal(barrier, inc=1, device_id=d, device_id_type=MESH)

    sent = []

    def send(src, dst, ss, rs, d):
        cp = pltpu.make_async_remote_copy(
            src_ref=src, dst_ref=dst, send_sem=ss, recv_sem=rs, device_id=d, device_id_type=MESH
        )
        cp.start()
        sent.append(cp)
        return cp

    order = [t for _, t in near.values()] + [t for _, t in far.values()] + [c * 2 + other, o]
    loads = []
    for n, t in enumerate(order):
        cols = pl.ds(pl.multiple_of(t * COLS, COLS), COLS)
        loads.append(pltpu.make_async_copy(coeffs.at[:, cols], raw.at[n], sl.at[n]))
        loads[n].start()

    energy = jnp.broadcast_to(energies[2:3, :], (TAIL, 128)).astype(BF16)
    near_in, far_in = {}, {}
    for n, t in enumerate(order):
        to = slabs.at[n] if n < 6 else rows.at[o, t % 2]
        loads[n].wait()
        for b in range(COLS // ABLK):
            cols = slice(b * ABLK, (b + 1) * ABLK)
            keep = screen[0, t * (COLS // ABLK) + b].astype(F32)
            kept = raw[n, :, cols] * jnp.full((VIRT, ABLK), keep, F32).astype(BF16)
            to[0:VIRT, cols] = kept
            to[VIRT:, cols] = energy
            if n == 3:
                also[o, 0:VIRT, cols] = kept
        if n == 0:
            pl.semaphore_wait(barrier, len(greet))
        if n < 4:
            key = list(near)[n]
            near_in[key] = send(slabs.at[n], rows.at[o, t % 2], sa.at[n], ra.at[n], near[key][0])
        elif n < 6:
            far_in[n - 4] = send(slabs.at[n], also.at[o], sr.at[n - 4], rr.at[n - 4], far[n - 4][0])
    to_partner = send(rows.at[o], rows.at[o], sa.at[4], ra.at[4], partner)
    also_in = send(slabs.at[0], also.at[o], sa.at[5], ra.at[5], partner)

    for half in (0, 1):
        vrow[half * 128 : (half + 1) * 128, :] = jnp.broadcast_to(
            energies[half : half + 1, :], (128, 128)
        ).T
    atom = lax.broadcasted_iota(jnp.int32, (3, 128), 1)
    for b in range(owner.shape[0]):
        spot = jnp.sum(jnp.where(atom == owner[b], positions[...], 0.0), axis=1, keepdims=True)
        where[0:3, b * ABLK : (b + 1) * ABLK] = jnp.broadcast_to(spot, (3, ABLK))
    pick = (
        lax.broadcasted_iota(jnp.int32, (CHUNK, 16 * CHUNK), 1) % CHUNK
        == lax.broadcasted_iota(jnp.int32, (CHUNK, 16 * CHUNK), 0)
    ).astype(F32).astype(BF16)

    def product(slot):
        r0, r1 = SLOTS[slot]
        first, second = (c + r0) % 4, (c + r1) % 4
        if slot in OPEN:
            first, second = jnp.minimum(first, second), jnp.maximum(first, second)
        lead = first * 2 + h
        for hc in (0, 1):
            s = dot_nt(rows[lead, 0, 0:VIRT], rows[second * 2 + hc, 0, 0:VIRT])
            s += dot_nt(rows[lead, 1, 0:VIRT], rows[second * 2 + hc, 1, 0:VIRT])
            part[slot, :, hc * VIRT : (hc + 1) * VIRT] = s.astype(BF16)

    def pass_on(n, came, src):
        came.wait_recv()
        piece = rows.at[src, h]
        return send(piece, piece, sf.at[n], rf.at[n], partner)

    plane_wait = {}

    def share_products(g):
        lo, hi = GROUPS[g]
        for j, (d, qd) in plane_peers.items():
            there = pl.ds(pl.multiple_of(qd * CHUNK, CHUNK), CHUNK)
            plane_wait[g, j] = send(
                part.at[lo:hi, there, :], plane_in.at[lo:hi, j], sp.at[g, j], rp.at[g, j], d
            )

    mine = pl.ds(pl.multiple_of(q * CHUNK, CHUNK), CHUNK)

    def block_id(slot):
        r0, r1 = SLOTS[slot]
        if r0 == r1:
            return (c + r0) % 4
        if slot in OPEN:
            return 8 + (c + r0) % 2
        return 4 + (c + r0) % 4

    def sum_plane(g):
        lo, hi = GROUPS[g]
        for j in plane_peers:
            plane_wait[g, j].wait_recv()
        for slot in range(lo, hi):
            plane_in[slot, 0] = part[slot, mine, :]
            terms = plane_in[slot].reshape(16 * CHUNK, 2 * VIRT)
            plane_sum[block_id(slot)] = dot_nn(pick, terms)

    to_partner.wait_recv()
    product(0)
    passed = []
    for n, ((way, flip), came) in enumerate(near_in.items()):
        src = chip(-side if way == flip else side) * 2 + (h + flip) % 2
        passed.append(pass_on(n, came, src))
    for cp in passed:
        cp.wait_recv()
    for slot in range(1, EARLY):
        product(slot)
    share_products(0)
    through = []
    for flip, came in far_in.items():
        came.wait_recv()
        src = chip(side) * 2 + (h + flip) % 2
        there = ((c + side + 8) % 4) * 2 + (h + flip) % 2
        through.append(send(also.at[src], rows.at[there, other], st.at[flip], rt.at[flip], buddy))
    passed = []
    for flip, came in enumerate(through):
        passed.append(pass_on(4 + flip, came, chip(2) * 2 + (other + flip) % 2))
    for cp in passed:
        cp.wait_recv()
    mid = []
    for n, src in enumerate((c, chip(side))):
        mid.append(send(
            rows.at[pl.ds(src * 2, 2), h], also.at[pl.ds(src * 2, 2)], sm.at[n], rm.at[n], buddy
        ))
    for slot in range(EARLY, NBLK):
        product(slot)
    share_products(1)
    sum_plane(0)
    sum_plane(1)

    def share_of(k):
        return (
            pl.ds((k // 4) * 5, 5),
            slice(None),
            pl.ds(pl.multiple_of((k % 4) * 128, 128), 128),
        )

    z_wait = {}
    for dz, (d, zd) in z_peers.items():
        z_wait[dz] = send(plane_sum.at[share_of(zd)], z_in.at[dz], sz.at[dz], rz.at[dz], d)
    for dz in z_peers:
        z_wait[dz].wait_recv()

    hc = (z % 4) // 2
    va = vrow[mine, :]
    vb = energies[pl.ds(z % 2, 1), :]
    lanes = pl.ds(pl.multiple_of((z % 4) * 128, 128), 128)
    for t in range(5):
        b = (z // 4) * 5 + t
        s = plane_sum[b, :, lanes]
        for dz in z_peers:
            s += z_in[dz, t]
        first = b % 4
        lead = first * 2 + h
        second = jnp.where(b < 4, first, jnp.where(b < 8, (first + 1) % 4, first + 2))
        ea = rows[lead, h, VIRT:, 0:128].astype(F32)
        eb = rows[second * 2 + hc, h, VIRT:, 0:128].astype(F32)
        z_amps[b, :, lanes] = (s / ((va - ea) + (vb - eb))).astype(BF16)
    y_wait = {}
    for dz, (d, _) in z_peers.items():
        y_wait[dz] = send(
            z_amps.at[share_of(z)], z_amps.at[share_of(z)], sy.at[dz], ry.at[dz], d
        )
    for dz in z_peers:
        y_wait[dz].wait_recv()

    here = pl.ds(pl.multiple_of(h * VIRT + q * CHUNK, CHUNK), CHUNK)
    for slot in range(NBLK - 1):
        amps[slot, here, :] = z_amps[block_id(slot)]
    g_wait = {}
    for g, (lo, hi) in enumerate(SPREADS):
        piece = amps.at[lo:hi, here, :]
        g_wait[g, 0] = send(piece, piece, sh.at[g, 0], rh.at[g, 0], partner)
        for j, (d, _) in plane_peers.items():
            g_wait[g, j] = send(piece, piece, sg.at[g, j], rg.at[g, j], d)

    def collect(g):
        lo, hi = SPREADS[g]
        out = [g_wait[g, 0]]
        for j in plane_peers:
            dx, dy = j // 4, j % 4
            src_q = ((x + 4 - dx) % 4) * 4 + (y + 4 - dy) % 4
            g_wait[g, j].wait_recv()
            piece = amps.at[lo:hi, pl.ds(pl.multiple_of(h * VIRT + src_q * CHUNK, CHUNK), CHUNK), :]
            out.append(send(piece, piece, sh.at[g, j], rh.at[g, j], partner))
        for cp in out:
            cp.wait_recv()

    def lay(n, slot, as_is):
        @pl.when(as_is)
        def _():
            turned[n] = amps[slot]

        @pl.when(jnp.logical_not(as_is))
        def _():
            turned[n] = amps[slot].T

    def gamma_rows(factors, hr, target, weights):
        span = pl.ds(pl.multiple_of(hr * VIRT, VIRT), VIRT)
        row_chip, send_to = target
        ro = row_chip * 2 + hr
        for k in (0, 1):
            acc = None
            for dot, ref, co in factors:
                for hcol in range(2):
                    half = slice(hcol * VIRT, (hcol + 1) * VIRT)
                    block = ref[span, half] if dot is dot_nn else ref[half, span]
                    src = co * 2 + hcol
                    term = dot(block, rows[src, h, 0:VIRT] if k == 0 else also[src, 0:VIRT])
                    acc = term if acc is None else acc + term
            out = acc.astype(BF16)
            m = rows[ro, h, 0:VIRT] if k == 0 else also[ro, 0:VIRT]
            weights[k] += jnp.sum(out.astype(F32) * m.astype(F32), axis=0, keepdims=True)
            t = o if k == 0 else buddy_o
            cols = pl.ds(pl.multiple_of(t * COLS, COLS), COLS)
            if send_to is None:
                gamma[:, cols] = out
            else:
                n, d = send_to
                gout[n + k] = out
                b_wait.append(send(gout.at[n + k], gamma.at[:, cols], sb.at[n + k], rb.at[n + k], d))

    b_wait = []
    weights = [jnp.zeros((1, COLS), F32), jnp.zeros((1, COLS), F32)]
    also_in.wait_recv()
    for cp in mid:
        cp.wait_recv()
    collect(0)
    lay(0, 3 + h, h == 1)
    lay(1, 6 + h, h == 0)
    lay(2, 5, chip(side) < 2)
    factors = (
        (dot_nn, turned.at[0], c),
        (dot_nn, amps.at[1 + h], chip(side)),
        (dot_nn, turned.at[1], chip(2)),
        (dot_nn, turned.at[2], chip(-side)),
    )
    for flip in (0, 1):
        hr = (h + flip) % 2
        gamma_rows(factors, hr, (chip(side), (flip * 2, near[0, flip][0])), weights)
    collect(1)
    collect(2)
    lay(3, 8, c < 2)
    factors = (
        (dot_nn, amps.at[0], c),
        (dot_nn, amps.at[3], chip(1)),
        (dot_nn, turned.at[3], chip(2)),
        (dot_tn, amps.at[4], chip(3)),
    )
    gamma_rows(factors, other, (c, (4, partner)), weights)
    gamma_rows(factors, h, (c, None), weights)

    for k in (0, 1):
        wmine[k * 8 : k * 8 + 8, :] = jnp.broadcast_to(weights[k], (8, COLS))
        wall[o, k * 8 : k * 8 + 8, :] = jnp.broadcast_to(weights[k], (8, COLS))
    w_wait = [
        send(wmine, wall.at[o], sw.at[n], rw.at[n], d) for n, d in enumerate(everyone)
    ]
    for cp in w_wait:
        cp.wait_recv()
    for t in range(8):
        cols = slice(t * COLS, (t + 1) * COLS)
        pair = ((t // 2 + 2 * (t % 2) - 1) % 4) * 2 + 1 - t % 2
        w = wall[t, 0:1, :] + wall[pair, 8:9, :]
        for i in range(3):
            for j in range(3):
                n = 3 * i + j
                virial[n : n + 1, cols] = where[i : i + 1, cols] * where[j : j + 1, cols] * w
    for cp in b_wait:
        cp.wait_recv()
    for cp in sent:
        cp.wait_send()


def body(coeffs, occ_energy, virt_energy, screen, owner, positions):
    occ_dev, virt, aux_dev = coeffs.shape
    energies = jnp.concatenate(
        [virt_energy.reshape(2, 128), jnp.broadcast_to(occ_energy[:, None], (1, 128))]
    ).astype(F32)
    vmem = pl.BlockSpec(memory_space=pltpu.VMEM)
    smem = pl.BlockSpec(memory_space=pltpu.SMEM)
    dma = pltpu.SemaphoreType.DMA
    gamma, virial = pl.pallas_call(
        kernel,
        out_shape=(
            jax.ShapeDtypeStruct((VIRT, aux_dev), BF16),
            jax.ShapeDtypeStruct((9, aux_dev), F32),
        ),
        in_specs=[smem, smem, pl.BlockSpec(memory_space=pl.ANY), vmem, vmem],
        out_specs=(vmem, vmem),
        scratch_shapes=[
            pltpu.VMEM((8, VIRT, COLS), BF16),
            pltpu.VMEM((6, VIRT + TAIL, COLS), BF16),
            pltpu.VMEM((8, 2, VIRT + TAIL, COLS), BF16),
            pltpu.VMEM((8, VIRT + TAIL, COLS), BF16),
            pltpu.VMEM((VIRT, 128), F32),
            pltpu.VMEM((NBLK, VIRT, 2 * VIRT), BF16),
            pltpu.VMEM((NBLK, 16, CHUNK, 2 * VIRT), BF16),
            pltpu.VMEM((NBLK, CHUNK, 2 * VIRT), F32),
            pltpu.VMEM((8, 5, CHUNK, 128), F32),
            pltpu.VMEM((NBLK, CHUNK, 2 * VIRT), BF16),
            pltpu.VMEM((NBLK, 2 * VIRT, 2 * VIRT), BF16),
            pltpu.VMEM((4, 2 * VIRT, 2 * VIRT), BF16),
            pltpu.VMEM((6, VIRT, COLS), BF16),
            pltpu.VMEM((16, COLS), F32),
            pltpu.VMEM((8, 16, COLS), F32),
            pltpu.VMEM((8, aux_dev), F32),
            dma((8,)), dma((6,)), dma((6,)), dma((2,)), dma((2,)), dma((2,)), dma((2,)),
            dma((6,)), dma((6,)), dma((2,)), dma((2,)),
            dma((2, 16)), dma((2, 16)), dma((8,)), dma((8,)), dma((8,)), dma((8,)),
            dma((3, 16)), dma((3, 16)), dma((3, 16)), dma((3, 16)),
            dma((6,)), dma((6,)), dma((7,)), dma((7,)),
        ],
        compiler_params=pltpu.CompilerParams(
            collective_id=0, has_side_effects=True, vmem_limit_bytes=60 * 1024 * 1024
        ),
    )(screen, owner, coeffs.reshape(VIRT, aux_dev), energies, positions)
    return gamma.reshape(occ_dev, virt, aux_dev), virial


def solution(mesh):
    placed = (P("occ", None, "aux"), P("occ"), P(), P("occ", "aux"), P("aux"), P())
    return jax.shard_map(
        body,
        mesh=mesh,
        in_specs=placed,
        out_specs=(P("occ", None, "aux"), P(None, "aux")),
        check_vma=False,
    )
```

```python
import jax
import jax.numpy as jnp
from jax import lax
from jax.experimental import pallas as pl
from jax.experimental.pallas import tpu as pltpu
from jax.sharding import PartitionSpec as P

MESH = pl.DeviceIdType.MESH
F32, BF16 = jnp.float32, jnp.bfloat16

ABLK = 128
VIRT = 256
COLS = 512
TAIL = 16
CHUNK = 16
NBLK = 10
PARTS = (slice(0, 256),)
EARLY = 6

SLOTS = ((0, 0), (1, 1), (3, 3), (0, 1), (3, 0), (1, 3), (1, 2), (2, 3), (0, 2), (2, 2))
OPEN = (5, 8)
GROUPS = ((0, EARLY), (EARLY, NBLK))
KEPT = (1, 2, 3, 4, 5, 6, 7, 0, 8)
SPREADS = ((0, 7), (7, 9))


def dot_nt(a, b):
    return lax.dot_general(a, b, (((1,), (1,)), ((), ())), preferred_element_type=F32)


def dot_nn(a, b):
    return lax.dot_general(a, b, (((1,), (0,)), ((), ())), preferred_element_type=F32)


def dot_tn(a, b):
    return lax.dot_general(a, b, (((0,), (0,)), ((), ())), preferred_element_type=F32)


def kernel(
    screen, owner, coeffs, energies, positions,
    gamma, virial,
    raw, slabs, rows, also, levels, vrow, part, plane_in, plane_sum, plane_out, z_in, z_amps, amps, turned, gout,
    wmine, wall, where,
    se, re, sl, sa, ra, sr, rr, st, rt, sf, rf, sm, rm, sp, rp, sz, rz, sy, ry, sg, rg, sh, rh, sb, rb, sw, rw,
):
    o = lax.axis_index("occ")
    a = lax.axis_index("aux")
    c, h = o // 2, o % 2
    y, zl, x = a % 4, (a // 4) % 2, a // 8
    z = c * 2 + zl
    q = x * 4 + y
    other = 1 - h
    side = 1 - 2 * h

    def chip(n):
        return (c + n + 8) % 4

    def at(x_, y_, z_, h_):
        return {"occ": (z_ // 2) * 2 + h_, "aux": (x_ * 2 + z_ % 2) * 4 + y_}

    partner = at(x, y, z, other)
    def on_ring(chip_, h_):
        return at(x, y, chip_ * 2 + zl, h_)

    buddy = on_ring(chip(-side), other)
    buddy_o = chip(-side) * 2 + other
    near = {}
    far = {}
    for flip in (0, 1):
        there = (h + flip) % 2
        for way in (0, 1):
            to = chip(side if way == 0 else -side)
            near[way, flip] = (on_ring(to, there), to * 2 + there)
        far[flip] = (on_ring(chip(2 * there - 1), there), chip(2) * 2 + 1 - there)
    plane_peers = {}
    for dx in range(4):
        for dy in range(4):
            if (dx, dy) != (0, 0):
                plane_peers[dx * 4 + dy] = (
                    at((x + dx) % 4, (y + dy) % 4, z, h),
                    ((x + dx) % 4) * 4 + (y + dy) % 4,
                )
    z_peers = {dz: (at(x, y, (z + dz) % 8, h), (z + dz) % 8) for dz in range(1, 8)}

    barrier = pltpu.get_barrier_semaphore()
    everyone = [partner, *(d for d, _ in near.values()), on_ring(chip(2), h), on_ring(chip(2), other)]
    greet = [*everyone]
    greet += [d for d, _ in plane_peers.values()]
    greet += [d for dz, (d, _) in z_peers.items() if dz % 2]
    for d in greet:
        pl.semaphore_signal(barrier, inc=1, device_id=d, device_id_type=MESH)

    sent = []

    def send(src, dst, ss, rs, d):
        cp = pltpu.make_async_remote_copy(
            src_ref=src, dst_ref=dst, send_sem=ss, recv_sem=rs, device_id=d, device_id_type=MESH
        )
        cp.start()
        sent.append(cp)
        return cp

    order = [t for _, t in near.values()] + [t for _, t in far.values()] + [c * 2 + other, o]
    loads = []
    for n, t in enumerate(order):
        cols = pl.ds(pl.multiple_of(t * COLS, COLS), COLS)
        loads.append(pltpu.make_async_copy(coeffs.at[:, cols], raw.at[n], sl.at[n]))
        loads[n].start()

    levels[o] = jnp.broadcast_to(energies[2:3, :], (TAIL, 128)).astype(BF16)
    near_in, far_in = {}, {}
    for n, t in enumerate(order):
        to = slabs.at[n] if n < 6 else rows.at[o, t % 2]
        loads[n].wait()
        for b in range(COLS // ABLK):
            cols = slice(b * ABLK, (b + 1) * ABLK)
            keep = screen[0, t * (COLS // ABLK) + b].astype(F32)
            kept = raw[n, :, cols] * jnp.full((VIRT, ABLK), keep, F32).astype(BF16)
            to[:, cols] = kept
            if n == 3:
                also[o, :, cols] = kept
        if n == 0:
            pl.semaphore_wait(barrier, len(greet))
        if n < 4:
            key = list(near)[n]
            near_in[key] = send(slabs.at[n], rows.at[o, t % 2], sa.at[n], ra.at[n], near[key][0])
        elif n < 6:
            for p, span in enumerate(PARTS):
                k = (n - 4) * 2 + p
                far_in[n - 4, p] = send(
                    slabs.at[n, span], also.at[o, span], sr.at[k], rr.at[k], far[n - 4][0]
                )
    level_in = [
        send(levels.at[o], levels.at[o], se.at[n], re.at[n], d) for n, d in enumerate(everyone)
    ]
    to_partner = send(rows.at[o], rows.at[o], sa.at[4], ra.at[4], partner)
    also_in = send(slabs.at[0], also.at[o], sa.at[5], ra.at[5], partner)

    for half in (0, 1):
        vrow[half * 128 : (half + 1) * 128, :] = jnp.broadcast_to(
            energies[half : half + 1, :], (128, 128)
        ).T
    atom = lax.broadcasted_iota(jnp.int32, (3, 128), 1)
    for b in range(owner.shape[0]):
        spot = jnp.sum(jnp.where(atom == owner[b], positions[...], 0.0), axis=1, keepdims=True)
        where[0:3, b * ABLK : (b + 1) * ABLK] = jnp.broadcast_to(spot, (3, ABLK))
    pick = (
        lax.broadcasted_iota(jnp.int32, (CHUNK, 16 * CHUNK), 1) % CHUNK
        == lax.broadcasted_iota(jnp.int32, (CHUNK, 16 * CHUNK), 0)
    ).astype(F32).astype(BF16)

    def product(slot):
        r0, r1 = SLOTS[slot]
        first, second = (c + r0) % 4, (c + r1) % 4
        if slot in OPEN:
            first, second = jnp.minimum(first, second), jnp.maximum(first, second)
        lead = first * 2 + h
        for hc in (0, 1):
            s = dot_nt(rows[lead, 0], rows[second * 2 + hc, 0])
            s += dot_nt(rows[lead, 1], rows[second * 2 + hc, 1])
            part[slot, :, hc * VIRT : (hc + 1) * VIRT] = s.astype(BF16)

    def pass_on(n, came, src, span=slice(0, VIRT)):
        came.wait_recv()
        piece = rows.at[src, h, span]
        return send(piece, piece, sf.at[n], rf.at[n], partner)

    plane_wait = {}

    def share_products(g):
        lo, hi = GROUPS[g]
        for j, (d, qd) in plane_peers.items():
            there = pl.ds(pl.multiple_of(qd * CHUNK, CHUNK), CHUNK)
            plane_wait[g, j] = send(
                part.at[lo:hi, there, :], plane_in.at[lo:hi, j], sp.at[g, j], rp.at[g, j], d
            )

    mine = pl.ds(pl.multiple_of(q * CHUNK, CHUNK), CHUNK)

    def block_id(slot):
        r0, r1 = SLOTS[slot]
        if r0 == r1:
            return (c + r0) % 4
        if slot in OPEN:
            return 8 + (c + r0) % 2
        return 4 + (c + r0) % 4

    def sum_plane(g):
        lo, hi = GROUPS[g]
        for j in plane_peers:
            plane_wait[g, j].wait_recv()
        for slot in range(lo, hi):
            plane_in[slot, 0] = part[slot, mine, :]
            terms = plane_in[slot].reshape(16 * CHUNK, 2 * VIRT)
            s = dot_nn(pick, terms)
            plane_sum[block_id(slot)] = s
            plane_out[block_id(slot)] = s.astype(BF16)

    to_partner.wait_recv()
    product(0)
    passed = []
    for n, ((way, flip), came) in enumerate(near_in.items()):
        src = chip(-side if way == flip else side) * 2 + (h + flip) % 2
        passed.append(pass_on(n, came, src))
    for cp in passed:
        cp.wait_recv()
    for slot in range(1, EARLY):
        product(slot)
    share_products(0)
    through = {}
    for p, span in enumerate(PARTS):
        for flip in (0, 1):
            far_in[flip, p].wait_recv()
            src = chip(side) * 2 + (h + flip) % 2
            k = flip * 2 + p
            through[flip, p] = send(
                also.at[src, span], rows.at[src, other, span], st.at[k], rt.at[k], buddy
            )
    passed = []
    for (flip, p), came in through.items():
        src = chip(2) * 2 + (other + flip) % 2
        passed.append(pass_on(4 + flip * 2 + p, came, src, PARTS[p]))
    for cp in passed:
        cp.wait_recv()

    def lend(n, src):
        return send(
            rows.at[pl.ds(src * 2, 2), h], also.at[pl.ds(src * 2, 2)], sm.at[n], rm.at[n], buddy
        )

    mid = [lend(0, c)]
    for g in (1,):
        for slot in range(*GROUPS[g]):
            product(slot)
        share_products(g)
    for g in (0, 1):
        sum_plane(g)

    def share_of(k):
        return (
            pl.ds((k // 4) * 5, 5),
            slice(None),
            pl.ds(pl.multiple_of((k % 4) * 128, 128), 128),
        )

    z_wait = {}
    for dz, (d, zd) in z_peers.items():
        z_wait[dz] = send(plane_out.at[share_of(zd)], z_in.at[dz], sz.at[dz], rz.at[dz], d)
    for dz in z_peers:
        z_wait[dz].wait_recv()

    for cp in level_in:
        cp.wait_recv()
    hc = (z % 4) // 2
    va = vrow[mine, :]
    vb = energies[pl.ds(z % 2, 1), :]
    lanes = pl.ds(pl.multiple_of((z % 4) * 128, 128), 128)
    for t in range(5):
        b = (z // 4) * 5 + t
        s = plane_sum[b, :, lanes]
        for dz in z_peers:
            s += z_in[dz, t].astype(F32)
        first = b % 4
        lead = first * 2 + h
        second = jnp.where(b < 4, first, jnp.where(b < 8, (first + 1) % 4, first + 2))
        ea = levels[lead].astype(F32)
        eb = levels[second * 2 + hc].astype(F32)
        z_amps[b, :, lanes] = (s / ((va - ea) + (vb - eb))).astype(BF16)
    y_wait = {}
    for dz, (d, _) in z_peers.items():
        y_wait[dz] = send(
            z_amps.at[share_of(z)], z_amps.at[share_of(z)], sy.at[dz], ry.at[dz], d
        )
    mid.append(lend(1, chip(side)))
    for dz in z_peers:
        y_wait[dz].wait_recv()

    here = pl.ds(pl.multiple_of(h * VIRT + q * CHUNK, CHUNK), CHUNK)
    for k, slot in enumerate(KEPT):
        amps[k, here, :] = z_amps[block_id(slot)]

    def piece(g, half, i, j):
        i, j = (i, j) if half == 0 else (j, i)
        src_q = ((x + 4 - i) % 4) * 4 + (y + 4 - j) % 4
        rows_ = pl.ds(pl.multiple_of(h * VIRT + src_q * CHUNK, CHUNK), CHUNK)
        return amps.at[slice(*SPREADS[g]), rows_, half * VIRT : (half + 1) * VIRT]

    def peer(half, i, j):
        i, j = (i, j) if half == 0 else (j, i)
        return plane_peers[i * 4 + j][0]

    g_wait, h_wait = {}, {0: [], 1: []}

    def spread(g, half, i):
        for j in (1, 3, 2):
            k = i * 4 + j
            g_wait[g, half, k] = send(
                piece(g, half, i, 0), piece(g, half, i, 0), sg.at[g, half, k], rg.at[g, half, k], peer(half, 0, j)
            )

    def to_other(g, half, i, j):
        k = i * 4 + j
        ref = piece(g, half, i, j)
        h_wait[g].append(send(ref, ref, sh.at[g, half, k], rh.at[g, half, k], partner))

    def begin(g):
        for i in (1, 3, 2):
            for half in (0, 1):
                k = i * 4
                ref = piece(g, half, 0, 0)
                g_wait[g, half, k] = send(ref, ref, sg.at[g, half, k], rg.at[g, half, k], peer(half, i, 0))
        for half in (0, 1):
            spread(g, half, 0)
            to_other(g, half, 0, 0)

    def relay(g):
        for i in (1, 3, 2):
            for half in (0, 1):
                g_wait[g, half, i * 4].wait_recv()
                spread(g, half, i)
                to_other(g, half, i, 0)

    def collect(g):
        for i in (0, 1, 3, 2):
            for j in (1, 3, 2):
                for half in (0, 1):
                    g_wait[g, half, i * 4 + j].wait_recv()
                    to_other(g, half, i, j)
        for cp in h_wait[g]:
            cp.wait_recv()

    def lay(n, slot, as_is):
        @pl.when(as_is)
        def _():
            turned[n] = amps[slot]

        @pl.when(jnp.logical_not(as_is))
        def _():
            turned[n] = amps[slot].T

    def gamma_rows(factors, hr, target, weights):
        span = pl.ds(pl.multiple_of(hr * VIRT, VIRT), VIRT)
        row_chip, send_to = target
        ro = row_chip * 2 + hr
        for k in (0, 1):
            acc = None
            for dot, ref, co in factors:
                for hcol in range(2):
                    half = slice(hcol * VIRT, (hcol + 1) * VIRT)
                    block = ref[span, half] if dot is dot_nn else ref[half, span]
                    src = co * 2 + hcol
                    term = dot(block, rows[src, h] if k == 0 else also[src])
                    acc = term if acc is None else acc + term
            out = acc.astype(BF16)
            m = rows[ro, h] if k == 0 else also[ro]
            weights[k] += jnp.sum(out.astype(F32) * m.astype(F32), axis=0, keepdims=True)
            t = o if k == 0 else buddy_o
            cols = pl.ds(pl.multiple_of(t * COLS, COLS), COLS)
            if send_to is None:
                gamma[:, cols] = out
            else:
                n, d = send_to
                gout[n + k] = out
                ready.append((n + k, cols, d))
                if n == 0:
                    send_ready()

    def send_ready():
        for n, cols, d in ready:
            b_wait.append(send(gout.at[n], gamma.at[:, cols], sb.at[n], rb.at[n], d))
        ready.clear()

    ready = []

    b_wait = []
    weights = [jnp.zeros((1, COLS), F32), jnp.zeros((1, COLS), F32)]
    begin(0)
    relay(0)
    begin(1)
    relay(1)
    also_in.wait_recv()
    for cp in mid:
        cp.wait_recv()
    collect(0)
    lay(0, 2 + h, h == 1)
    lay(1, 5 + h, h == 0)
    lay(2, 4, chip(side) < 2)
    factors = (
        (dot_nn, turned.at[0], c),
        (dot_nn, amps.at[h], chip(side)),
        (dot_nn, turned.at[1], chip(2)),
        (dot_nn, turned.at[2], chip(-side)),
    )
    for flip in (0, 1):
        hr = (h + flip) % 2
        gamma_rows(factors, hr, (chip(side), (flip * 2, near[0, flip][0])), weights)
    later = [*ready]
    ready.clear()
    collect(1)
    lay(3, 8, c < 2)
    factors = (
        (dot_nn, amps.at[7], c),
        (dot_nn, amps.at[2], chip(1)),
        (dot_nn, turned.at[3], chip(2)),
        (dot_tn, amps.at[3], chip(3)),
    )
    gamma_rows(factors, other, (c, (4, partner)), weights)
    send_ready()
    gamma_rows(factors, h, (c, None), weights)

    for k in (0, 1):
        wmine[k * 8 : k * 8 + 8, :] = jnp.broadcast_to(weights[k], (8, COLS))
        wall[o, k * 8 : k * 8 + 8, :] = jnp.broadcast_to(weights[k], (8, COLS))
    w_wait = [
        send(wmine, wall.at[o], sw.at[n], rw.at[n], d) for n, d in enumerate(everyone)
    ]
    ready.extend(later)
    send_ready()
    for cp in w_wait:
        cp.wait_recv()
    for t in range(8):
        cols = slice(t * COLS, (t + 1) * COLS)
        pair = ((t // 2 + 2 * (t % 2) - 1) % 4) * 2 + 1 - t % 2
        w = wall[t, 0:1, :] + wall[pair, 8:9, :]
        for i in range(3):
            for j in range(3):
                n = 3 * i + j
                virial[n : n + 1, cols] = where[i : i + 1, cols] * where[j : j + 1, cols] * w
    for cp in b_wait:
        cp.wait_recv()
    for cp in sent:
        cp.wait_send()


def body(coeffs, occ_energy, virt_energy, screen, owner, positions):
    occ_dev, virt, aux_dev = coeffs.shape
    energies = jnp.concatenate(
        [virt_energy.reshape(2, 128), jnp.broadcast_to(occ_energy[:, None], (1, 128))]
    ).astype(F32)
    vmem = pl.BlockSpec(memory_space=pltpu.VMEM)
    smem = pl.BlockSpec(memory_space=pltpu.SMEM)
    dma = pltpu.SemaphoreType.DMA
    gamma, virial = pl.pallas_call(
        kernel,
        out_shape=(
            jax.ShapeDtypeStruct((VIRT, aux_dev), BF16),
            jax.ShapeDtypeStruct((9, aux_dev), F32),
        ),
        in_specs=[smem, smem, pl.BlockSpec(memory_space=pl.ANY), vmem, vmem],
        out_specs=(vmem, vmem),
        scratch_shapes=[
            pltpu.VMEM((8, VIRT, COLS), BF16),
            pltpu.VMEM((6, VIRT, COLS), BF16),
            pltpu.VMEM((8, 2, VIRT, COLS), BF16),
            pltpu.VMEM((8, VIRT, COLS), BF16),
            pltpu.VMEM((8, TAIL, 128), BF16),
            pltpu.VMEM((VIRT, 128), F32),
            pltpu.VMEM((NBLK, VIRT, 2 * VIRT), BF16),
            pltpu.VMEM((NBLK, 16, CHUNK, 2 * VIRT), BF16),
            pltpu.VMEM((NBLK, CHUNK, 2 * VIRT), F32),
            pltpu.VMEM((NBLK, CHUNK, 2 * VIRT), BF16),
            pltpu.VMEM((8, 5, CHUNK, 128), BF16),
            pltpu.VMEM((NBLK, CHUNK, 2 * VIRT), BF16),
            pltpu.VMEM((NBLK - 1, 2 * VIRT, 2 * VIRT), BF16),
            pltpu.VMEM((4, 2 * VIRT, 2 * VIRT), BF16),
            pltpu.VMEM((6, VIRT, COLS), BF16),
            pltpu.VMEM((16, COLS), F32),
            pltpu.VMEM((8, 16, COLS), F32),
            pltpu.VMEM((8, aux_dev), F32),
            dma((7,)), dma((7,)), dma((8,)), dma((6,)), dma((6,)), dma((4,)), dma((4,)), dma((4,)), dma((4,)),
            dma((8,)), dma((8,)), dma((2,)), dma((2,)),
            dma((3, 16)), dma((3, 16)), dma((8,)), dma((8,)), dma((8,)), dma((8,)),
            dma((2, 2, 16)), dma((2, 2, 16)), dma((2, 2, 16)), dma((2, 2, 16)),
            dma((6,)), dma((6,)), dma((7,)), dma((7,)),
        ],
        compiler_params=pltpu.CompilerParams(
            collective_id=0, has_side_effects=True, vmem_limit_bytes=60 * 1024 * 1024
        ),
    )(screen, owner, coeffs.reshape(VIRT, aux_dev), energies, positions)
    return gamma.reshape(occ_dev, virt, aux_dev), virial


def solution(mesh):
    placed = (P("occ", None, "aux"), P("occ"), P(), P("occ", "aux"), P("aux"), P())
    return jax.shard_map(
        body,
        mesh=mesh,
        in_specs=placed,
        out_specs=(P("occ", None, "aux"), P(None, "aux")),
        check_vma=False,
    )
```

```python
import jax
import jax.numpy as jnp
from jax import lax
from jax.experimental import pallas as pl
from jax.experimental.pallas import tpu as pltpu
from jax.sharding import PartitionSpec as P

MESH = pl.DeviceIdType.MESH
F32, BF16 = jnp.float32, jnp.bfloat16

ABLK = 128
VIRT = 256
COLS = 512
TAIL = 16
CHUNK = 16
NBLK = 10
PARTS = (slice(0, 256),)
EARLY = 6

SLOTS = ((0, 0), (1, 1), (3, 3), (0, 1), (3, 0), (1, 3), (1, 2), (2, 3), (0, 2), (2, 2))
OPEN = (5, 8)
GROUPS = ((0, EARLY), (EARLY, NBLK))
KEPT = (1, 2, 3, 4, 5, 6, 7, 0, 8)
SPREADS = ((0, 7), (7, 9))


def dot_nt(a, b):
    return lax.dot_general(a, b, (((1,), (1,)), ((), ())), preferred_element_type=F32)


def dot_nn(a, b):
    return lax.dot_general(a, b, (((1,), (0,)), ((), ())), preferred_element_type=F32)


def dot_tn(a, b):
    return lax.dot_general(a, b, (((0,), (0,)), ((), ())), preferred_element_type=F32)


def kernel(
    screen, owner, coeffs, energies, positions,
    gamma, virial,
    raw, slabs, rows, also, levels, vrow, part, plane_in, plane_sum, plane_out, z_in, z_amps, amps, turned, gout,
    wmine, wall, where,
    se, re, sl, sa, ra, sr, rr, st, rt, sf, rf, sm, rm, sp, rp, sz, rz, sy, ry, sg, rg, sh, rh, sb, rb, sw, rw,
):
    o = lax.axis_index("occ")
    a = lax.axis_index("aux")
    c, h = o // 2, o % 2
    y, zl, x = a % 4, (a // 4) % 2, a // 8
    z = c * 2 + zl
    q = x * 4 + y
    other = 1 - h
    side = 1 - 2 * h

    def chip(n):
        return (c + n + 8) % 4

    def at(x_, y_, z_, h_):
        return {"occ": (z_ // 2) * 2 + h_, "aux": (x_ * 2 + z_ % 2) * 4 + y_}

    partner = at(x, y, z, other)
    def on_ring(chip_, h_):
        return at(x, y, chip_ * 2 + zl, h_)

    buddy = on_ring(chip(-side), other)
    buddy_o = chip(-side) * 2 + other
    near = {}
    far = {}
    for flip in (0, 1):
        there = (h + flip) % 2
        for way in (0, 1):
            to = chip(side if way == 0 else -side)
            near[way, flip] = (on_ring(to, there), to * 2 + there)
        far[flip] = (on_ring(chip(2 * there - 1), there), chip(2) * 2 + 1 - there)
    plane_peers = {}
    for dx in range(4):
        for dy in range(4):
            if (dx, dy) != (0, 0):
                plane_peers[dx * 4 + dy] = (
                    at((x + dx) % 4, (y + dy) % 4, z, h),
                    ((x + dx) % 4) * 4 + (y + dy) % 4,
                )
    z_peers = {dz: (at(x, y, (z + dz) % 8, h), (z + dz) % 8) for dz in range(1, 8)}

    barrier = pltpu.get_barrier_semaphore()
    everyone = [partner, *(d for d, _ in near.values()), on_ring(chip(2), h), on_ring(chip(2), other)]
    greet = [*everyone]
    greet += [d for d, _ in plane_peers.values()]
    greet += [d for dz, (d, _) in z_peers.items() if dz % 2]
    for d in greet:
        pl.semaphore_signal(barrier, inc=1, device_id=d, device_id_type=MESH)

    sent = []

    def send(src, dst, ss, rs, d):
        cp = pltpu.make_async_remote_copy(
            src_ref=src, dst_ref=dst, send_sem=ss, recv_sem=rs, device_id=d, device_id_type=MESH
        )
        cp.start()
        sent.append(cp)
        return cp

    order = [t for _, t in near.values()] + [t for _, t in far.values()] + [c * 2 + other, o]
    loads = []
    for n, t in enumerate(order):
        cols = pl.ds(pl.multiple_of(t * COLS, COLS), COLS)
        loads.append(pltpu.make_async_copy(coeffs.at[:, cols], raw.at[n], sl.at[n]))
        loads[n].start()

    levels[o] = jnp.broadcast_to(energies[2:3, :], (TAIL, 128)).astype(BF16)
    near_in, far_in = {}, {}
    for n, t in enumerate(order):
        to = slabs.at[n] if n < 6 else rows.at[o, t % 2]
        loads[n].wait()
        for b in range(COLS // ABLK):
            cols = slice(b * ABLK, (b + 1) * ABLK)
            keep = screen[0, t * (COLS // ABLK) + b].astype(F32)
            kept = raw[n, :, cols] * jnp.full((VIRT, ABLK), keep, F32).astype(BF16)
            to[:, cols] = kept
            if n == 3:
                also[o, :, cols] = kept
        if n == 0:
            pl.semaphore_wait(barrier, len(greet))
        if n < 4:
            key = list(near)[n]
            near_in[key] = send(slabs.at[n], rows.at[o, t % 2], sa.at[n], ra.at[n], near[key][0])
        elif n < 6:
            for p, span in enumerate(PARTS):
                k = (n - 4) * 2 + p
                far_in[n - 4, p] = send(
                    slabs.at[n, span], also.at[o, span], sr.at[k], rr.at[k], far[n - 4][0]
                )
    level_in = [
        send(levels.at[o], levels.at[o], se.at[n], re.at[n], d) for n, d in enumerate(everyone)
    ]
    to_partner = send(rows.at[o], rows.at[o], sa.at[4], ra.at[4], partner)
    also_in = send(slabs.at[0], also.at[o], sa.at[5], ra.at[5], partner)

    for half in (0, 1):
        vrow[half * 128 : (half + 1) * 128, :] = jnp.broadcast_to(
            energies[half : half + 1, :], (128, 128)
        ).T
    atom = lax.broadcasted_iota(jnp.int32, (3, 128), 1)
    for b in range(owner.shape[0]):
        spot = jnp.sum(jnp.where(atom == owner[b], positions[...], 0.0), axis=1, keepdims=True)
        where[0:3, b * ABLK : (b + 1) * ABLK] = jnp.broadcast_to(spot, (3, ABLK))
    pick = (
        lax.broadcasted_iota(jnp.int32, (CHUNK, 16 * CHUNK), 1) % CHUNK
        == lax.broadcasted_iota(jnp.int32, (CHUNK, 16 * CHUNK), 0)
    ).astype(F32).astype(BF16)

    def product(slot):
        r0, r1 = SLOTS[slot]
        first, second = (c + r0) % 4, (c + r1) % 4
        if slot in OPEN:
            first, second = jnp.minimum(first, second), jnp.maximum(first, second)
        lead = first * 2 + h
        for hc in (0, 1):
            s = dot_nt(rows[lead, 0], rows[second * 2 + hc, 0])
            s += dot_nt(rows[lead, 1], rows[second * 2 + hc, 1])
            part[slot, :, hc * VIRT : (hc + 1) * VIRT] = s.astype(BF16)

    def pass_on(n, came, src, span=slice(0, VIRT)):
        came.wait_recv()
        piece = rows.at[src, h, span]
        return send(piece, piece, sf.at[n], rf.at[n], partner)

    plane_wait = {}

    def share_products(g):
        lo, hi = GROUPS[g]
        for j, (d, qd) in plane_peers.items():
            there = pl.ds(pl.multiple_of(qd * CHUNK, CHUNK), CHUNK)
            plane_wait[g, j] = send(
                part.at[lo:hi, there, :], plane_in.at[lo:hi, j], sp.at[g, j], rp.at[g, j], d
            )

    mine = pl.ds(pl.multiple_of(q * CHUNK, CHUNK), CHUNK)

    def block_id(slot):
        r0, r1 = SLOTS[slot]
        if r0 == r1:
            return (c + r0) % 4
        if slot in OPEN:
            return 8 + (c + r0) % 2
        return 4 + (c + r0) % 4

    def sum_plane(g):
        lo, hi = GROUPS[g]
        for j in plane_peers:
            plane_wait[g, j].wait_recv()
        for slot in range(lo, hi):
            plane_in[slot, 0] = part[slot, mine, :]
            terms = plane_in[slot].reshape(16 * CHUNK, 2 * VIRT)
            s = dot_nn(pick, terms)
            plane_sum[block_id(slot)] = s
            plane_out[block_id(slot)] = s.astype(BF16)

    to_partner.wait_recv()
    product(0)
    passed = []
    for n, ((way, flip), came) in enumerate(near_in.items()):
        src = chip(-side if way == flip else side) * 2 + (h + flip) % 2
        passed.append(pass_on(n, came, src))
    for cp in passed:
        cp.wait_recv()
    for slot in range(1, EARLY):
        product(slot)
    share_products(0)
    through = {}
    for p, span in enumerate(PARTS):
        for flip in (0, 1):
            far_in[flip, p].wait_recv()
            src = chip(side) * 2 + (h + flip) % 2
            k = flip * 2 + p
            through[flip, p] = send(
                also.at[src, span], rows.at[src, other, span], st.at[k], rt.at[k], buddy
            )
    passed = []
    for (flip, p), came in through.items():
        src = chip(2) * 2 + (other + flip) % 2
        passed.append(pass_on(4 + flip * 2 + p, came, src, PARTS[p]))
    for cp in passed:
        cp.wait_recv()

    def lend(n, src):
        return send(
            rows.at[pl.ds(src * 2, 2), h], also.at[pl.ds(src * 2, 2)], sm.at[n], rm.at[n], buddy
        )

    mid = [lend(0, c)]
    for g in (1,):
        for slot in range(*GROUPS[g]):
            product(slot)
        share_products(g)
    for g in (0, 1):
        sum_plane(g)

    def share_of(k):
        return (
            pl.ds((k // 4) * 5, 5),
            slice(None),
            pl.ds(pl.multiple_of((k % 4) * 128, 128), 128),
        )

    z_wait = {}
    for dz, (d, zd) in z_peers.items():
        z_wait[dz] = send(plane_out.at[share_of(zd)], z_in.at[dz], sz.at[dz], rz.at[dz], d)
    for dz in z_peers:
        z_wait[dz].wait_recv()

    for cp in level_in:
        cp.wait_recv()
    hc = (z % 4) // 2
    va = vrow[mine, :]
    vb = energies[pl.ds(z % 2, 1), :]
    lanes = pl.ds(pl.multiple_of((z % 4) * 128, 128), 128)
    for t in range(5):
        b = (z // 4) * 5 + t
        s = plane_sum[b, :, lanes]
        for dz in z_peers:
            s += z_in[dz, t].astype(F32)
        first = b % 4
        lead = first * 2 + h
        second = jnp.where(b < 4, first, jnp.where(b < 8, (first + 1) % 4, first + 2))
        ea = levels[lead].astype(F32)
        eb = levels[second * 2 + hc].astype(F32)
        z_amps[b, :, lanes] = (s / ((va - ea) + (vb - eb))).astype(BF16)
    y_wait = {}
    for dz, (d, _) in z_peers.items():
        y_wait[dz] = send(
            z_amps.at[share_of(z)], z_amps.at[share_of(z)], sy.at[dz], ry.at[dz], d
        )
    mid.append(lend(1, chip(side)))
    for dz in z_peers:
        y_wait[dz].wait_recv()

    here = pl.ds(pl.multiple_of(h * VIRT + q * CHUNK, CHUNK), CHUNK)
    for k, slot in enumerate(KEPT):
        amps[k, here, :] = z_amps[block_id(slot)]

    def piece(g, half, i, j):
        i, j = (i, j) if half == 0 else (j, i)
        src_q = ((x + 4 - i) % 4) * 4 + (y + 4 - j) % 4
        rows_ = pl.ds(pl.multiple_of(h * VIRT + src_q * CHUNK, CHUNK), CHUNK)
        return amps.at[slice(*SPREADS[g]), rows_, half * VIRT : (half + 1) * VIRT]

    def peer(half, i, j):
        i, j = (i, j) if half == 0 else (j, i)
        return plane_peers[i * 4 + j][0]

    g_wait, h_wait = {}, {0: [], 1: []}

    def spread(g, half, i):
        for j in (1, 3, 2):
            k = i * 4 + j
            g_wait[g, half, k] = send(
                piece(g, half, i, 0), piece(g, half, i, 0), sg.at[g, half, k], rg.at[g, half, k], peer(half, 0, j)
            )

    def to_other(g, n, rows_, cols):
        ref = amps.at[slice(*SPREADS[g]), rows_, cols]
        h_wait[g].append(send(ref, ref, sh.at[g, n], rh.at[g, n], partner))

    def begin(g):
        for i in (1, 3, 2):
            for half in (0, 1):
                k = i * 4
                ref = piece(g, half, 0, 0)
                g_wait[g, half, k] = send(ref, ref, sg.at[g, half, k], rg.at[g, half, k], peer(half, i, 0))
        for half in (0, 1):
            spread(g, half, 0)

    def relay(g):
        for i in (1, 3, 2):
            for half in (0, 1):
                g_wait[g, half, i * 4].wait_recv()
                spread(g, half, i)

    def collect(g):
        for i in (0, 1, 3, 2):
            for j in (1, 3, 2):
                g_wait[g, 0, i * 4 + j].wait_recv()
            first = pl.multiple_of(h * VIRT + ((x + 4 - i) % 4) * 4 * CHUNK, 4 * CHUNK)
            to_other(g, i, pl.ds(first, 4 * CHUNK), slice(0, VIRT))
        for i in (0, 1, 3, 2):
            for j in (1, 3, 2):
                g_wait[g, 1, i * 4 + j].wait_recv()
        own = pl.ds(pl.multiple_of(h * VIRT, VIRT), VIRT)
        to_other(g, 4, own, slice(VIRT, 2 * VIRT))
        for cp in h_wait[g]:
            cp.wait_recv()

    def lay(n, slot, as_is):
        @pl.when(as_is)
        def _():
            turned[n] = amps[slot]

        @pl.when(jnp.logical_not(as_is))
        def _():
            turned[n] = amps[slot].T

    def gamma_rows(factors, hr, target, weights):
        span = pl.ds(pl.multiple_of(hr * VIRT, VIRT), VIRT)
        row_chip, send_to = target
        ro = row_chip * 2 + hr
        for k in (0, 1):
            acc = None
            for dot, ref, co in factors:
                for hcol in range(2):
                    half = slice(hcol * VIRT, (hcol + 1) * VIRT)
                    block = ref[span, half] if dot is dot_nn else ref[half, span]
                    src = co * 2 + hcol
                    term = dot(block, rows[src, h] if k == 0 else also[src])
                    acc = term if acc is None else acc + term
            out = acc.astype(BF16)
            m = rows[ro, h] if k == 0 else also[ro]
            weights[k] += jnp.sum(out.astype(F32) * m.astype(F32), axis=0, keepdims=True)
            t = o if k == 0 else buddy_o
            cols = pl.ds(pl.multiple_of(t * COLS, COLS), COLS)
            if send_to is None:
                gamma[:, cols] = out
            else:
                n, d = send_to
                gout[n + k] = out
                ready.append((n + k, cols, d))
                if n == 0:
                    send_ready()

    def send_ready():
        for n, cols, d in ready:
            b_wait.append(send(gout.at[n], gamma.at[:, cols], sb.at[n], rb.at[n], d))
        ready.clear()

    ready = []

    b_wait = []
    weights = [jnp.zeros((1, COLS), F32), jnp.zeros((1, COLS), F32)]
    begin(0)
    relay(0)
    begin(1)
    relay(1)
    also_in.wait_recv()
    for cp in mid:
        cp.wait_recv()
    collect(0)
    lay(0, 2 + h, h == 1)
    lay(1, 5 + h, h == 0)
    lay(2, 4, chip(side) < 2)
    factors = (
        (dot_nn, turned.at[0], c),
        (dot_nn, amps.at[h], chip(side)),
        (dot_nn, turned.at[1], chip(2)),
        (dot_nn, turned.at[2], chip(-side)),
    )
    for flip in (0, 1):
        hr = (h + flip) % 2
        gamma_rows(factors, hr, (chip(side), (flip * 2, near[0, flip][0])), weights)
    later = [*ready]
    ready.clear()
    collect(1)
    lay(3, 8, c < 2)
    factors = (
        (dot_nn, amps.at[7], c),
        (dot_nn, amps.at[2], chip(1)),
        (dot_nn, turned.at[3], chip(2)),
        (dot_tn, amps.at[3], chip(3)),
    )
    gamma_rows(factors, other, (c, (4, partner)), weights)
    send_ready()
    gamma_rows(factors, h, (c, None), weights)

    for k in (0, 1):
        wmine[k * 8 : k * 8 + 8, :] = jnp.broadcast_to(weights[k], (8, COLS))
        wall[o, k * 8 : k * 8 + 8, :] = jnp.broadcast_to(weights[k], (8, COLS))
    w_wait = [
        send(wmine, wall.at[o], sw.at[n], rw.at[n], d) for n, d in enumerate(everyone)
    ]
    ready.extend(later)
    send_ready()
    for cp in w_wait:
        cp.wait_recv()
    for t in range(8):
        cols = slice(t * COLS, (t + 1) * COLS)
        pair = ((t // 2 + 2 * (t % 2) - 1) % 4) * 2 + 1 - t % 2
        w = wall[t, 0:1, :] + wall[pair, 8:9, :]
        for i in range(3):
            for j in range(3):
                n = 3 * i + j
                virial[n : n + 1, cols] = where[i : i + 1, cols] * where[j : j + 1, cols] * w
    for cp in b_wait:
        cp.wait_recv()
    for cp in sent:
        cp.wait_send()


def write_out(gamma_in, virial_in, gamma, virial, sem):
    copies = [
        pltpu.make_async_copy(gamma_in, gamma, sem.at[0]),
        pltpu.make_async_copy(virial_in, virial, sem.at[1]),
    ]
    for cp in copies:
        cp.start()
    for cp in copies:
        cp.wait()


def body(coeffs, occ_energy, virt_energy, screen, owner, positions):
    occ_dev, virt, aux_dev = coeffs.shape
    energies = jnp.concatenate(
        [virt_energy.reshape(2, 128), jnp.broadcast_to(occ_energy[:, None], (1, 128))]
    ).astype(F32)
    vmem = pl.BlockSpec(memory_space=pltpu.VMEM)
    smem = pl.BlockSpec(memory_space=pltpu.SMEM)
    dma = pltpu.SemaphoreType.DMA
    gamma, virial = pl.pallas_call(
        kernel,
        out_shape=(pltpu.VMEM((VIRT, aux_dev), BF16), pltpu.VMEM((9, aux_dev), F32)),
        in_specs=[smem, smem, pl.BlockSpec(memory_space=pltpu.HBM), vmem, vmem],
        out_specs=(vmem, vmem),
        scratch_shapes=[
            pltpu.VMEM((8, VIRT, COLS), BF16),
            pltpu.VMEM((6, VIRT, COLS), BF16),
            pltpu.VMEM((8, 2, VIRT, COLS), BF16),
            pltpu.VMEM((8, VIRT, COLS), BF16),
            pltpu.VMEM((8, TAIL, 128), BF16),
            pltpu.VMEM((VIRT, 128), F32),
            pltpu.VMEM((NBLK, VIRT, 2 * VIRT), BF16),
            pltpu.VMEM((NBLK, 16, CHUNK, 2 * VIRT), BF16),
            pltpu.VMEM((NBLK, CHUNK, 2 * VIRT), F32),
            pltpu.VMEM((NBLK, CHUNK, 2 * VIRT), BF16),
            pltpu.VMEM((8, 5, CHUNK, 128), BF16),
            pltpu.VMEM((NBLK, CHUNK, 2 * VIRT), BF16),
            pltpu.VMEM((NBLK - 1, 2 * VIRT, 2 * VIRT), BF16),
            pltpu.VMEM((4, 2 * VIRT, 2 * VIRT), BF16),
            pltpu.VMEM((6, VIRT, COLS), BF16),
            pltpu.VMEM((16, COLS), F32),
            pltpu.VMEM((8, 16, COLS), F32),
            pltpu.VMEM((8, aux_dev), F32),
            dma((7,)), dma((7,)), dma((8,)), dma((6,)), dma((6,)), dma((4,)), dma((4,)), dma((4,)), dma((4,)),
            dma((8,)), dma((8,)), dma((2,)), dma((2,)),
            dma((3, 16)), dma((3, 16)), dma((8,)), dma((8,)), dma((8,)), dma((8,)),
            dma((2, 2, 16)), dma((2, 2, 16)), dma((2, 5)), dma((2, 5)),
            dma((6,)), dma((6,)), dma((7,)), dma((7,)),
        ],
        compiler_params=pltpu.CompilerParams(
            collective_id=0, has_side_effects=True, vmem_limit_bytes=64684032
        ),
    )(screen, owner, coeffs.reshape(VIRT, aux_dev), energies, positions)
    gamma, virial = pl.pallas_call(
        write_out,
        out_shape=(
            jax.ShapeDtypeStruct((VIRT, aux_dev), BF16),
            jax.ShapeDtypeStruct((9, aux_dev), F32),
        ),
        in_specs=[pl.BlockSpec(memory_space=pl.ANY)] * 2,
        out_specs=(pl.BlockSpec(memory_space=pl.ANY),) * 2,
        scratch_shapes=[dma((2,))],
        compiler_params=pltpu.CompilerParams(vmem_limit_bytes=1024 * 1024),
    )(gamma, virial)
    return gamma.reshape(occ_dev, virt, aux_dev), virial


def solution(mesh):
    placed = (P("occ", None, "aux"), P("occ"), P(), P("occ", "aux"), P("aux"), P())
    return jax.shard_map(
        body,
        mesh=mesh,
        in_specs=placed,
        out_specs=(P("occ", None, "aux"), P(None, "aux")),
        check_vma=False,
    )
```

```python
import jax
import jax.numpy as jnp
from jax import lax
from jax.experimental import pallas as pl
from jax.experimental.pallas import tpu as pltpu
from jax.sharding import PartitionSpec as P

MESH = pl.DeviceIdType.MESH
F32, BF16 = jnp.float32, jnp.bfloat16

ABLK = 128
VIRT = 256
COLS = 512
TAIL = 16
CHUNK = 16
NBLK = 10
PARTS = (slice(0, 256),)
EARLY = 6

SLOTS = ((0, 0), (1, 1), (3, 3), (0, 1), (3, 0), (1, 3), (1, 2), (2, 3), (0, 2), (2, 2))
OPEN = (5, 8)
GROUPS = ((0, 1), (1, 3), (3, EARLY), (EARLY, 8), (8, NBLK))
KEPT = (1, 2, 3, 4, 5, 6, 7, 0, 8)
SPREADS = ((0, 7), (7, 9))


def dot_nt(a, b):
    return lax.dot_general(a, b, (((1,), (1,)), ((), ())), preferred_element_type=F32)


def dot_nn(a, b):
    return lax.dot_general(a, b, (((1,), (0,)), ((), ())), preferred_element_type=F32)


def dot_tn(a, b):
    return lax.dot_general(a, b, (((0,), (0,)), ((), ())), preferred_element_type=F32)


def kernel(
    screen, owner, coeffs, energies, positions,
    gamma, virial,
    raw, slabs, rows, also, levels, vrow, part, plane_in, plane_sum, plane_out, z_in, z_amps, amps, turned, gout,
    wmine, wall, where,
    se, re, sl, sa, ra, sr, rr, st, rt, sf, rf, sm, rm, sp, rp, sz, rz, sy, ry, sg, rg, sh, rh, sb, rb, sw, rw,
):
    o = lax.axis_index("occ")
    a = lax.axis_index("aux")
    c, h = o // 2, o % 2
    y, zl, x = a % 4, (a // 4) % 2, a // 8
    z = c * 2 + zl
    q = x * 4 + y
    other = 1 - h
    side = 1 - 2 * h

    def chip(n):
        return (c + n + 8) % 4

    def at(x_, y_, z_, h_):
        return {"occ": (z_ // 2) * 2 + h_, "aux": (x_ * 2 + z_ % 2) * 4 + y_}

    partner = at(x, y, z, other)
    def on_ring(chip_, h_):
        return at(x, y, chip_ * 2 + zl, h_)

    buddy = on_ring(chip(-side), other)
    buddy_o = chip(-side) * 2 + other
    near = {}
    far = {}
    for flip in (0, 1):
        there = (h + flip) % 2
        for way in (0, 1):
            to = chip(side if way == 0 else -side)
            near[way, flip] = (on_ring(to, there), to * 2 + there)
        far[flip] = (on_ring(chip(2 * there - 1), there), chip(2) * 2 + 1 - there)
    plane_peers = {}
    for dx in range(4):
        for dy in range(4):
            if (dx, dy) != (0, 0):
                plane_peers[dx * 4 + dy] = (
                    at((x + dx) % 4, (y + dy) % 4, z, h),
                    ((x + dx) % 4) * 4 + (y + dy) % 4,
                )
    z_peers = {dz: (at(x, y, (z + dz) % 8, h), (z + dz) % 8) for dz in range(1, 8)}

    barrier = pltpu.get_barrier_semaphore()
    everyone = [partner, *(d for d, _ in near.values()), on_ring(chip(2), h), on_ring(chip(2), other)]
    greet = [*everyone]
    greet += [d for d, _ in plane_peers.values()]
    greet += [d for dz, (d, _) in z_peers.items() if dz % 2]
    for d in greet:
        pl.semaphore_signal(barrier, inc=1, device_id=d, device_id_type=MESH)

    sent = []

    def send(src, dst, ss, rs, d):
        cp = pltpu.make_async_remote_copy(
            src_ref=src, dst_ref=dst, send_sem=ss, recv_sem=rs, device_id=d, device_id_type=MESH
        )
        cp.start()
        sent.append(cp)
        return cp

    order = [t for _, t in near.values()] + [t for _, t in far.values()] + [c * 2 + other, o]
    loads = []
    for n, t in enumerate(order):
        cols = pl.ds(pl.multiple_of(t * COLS, COLS), COLS)
        loads.append(pltpu.make_async_copy(coeffs.at[:, cols], raw.at[n], sl.at[n]))
        loads[n].start()

    levels[o] = jnp.broadcast_to(energies[2:3, :], (TAIL, 128)).astype(BF16)
    near_in, far_in = {}, {}
    for n, t in enumerate(order):
        to = slabs.at[n] if n < 6 else rows.at[o, t % 2]
        loads[n].wait()
        for b in range(COLS // ABLK):
            cols = slice(b * ABLK, (b + 1) * ABLK)
            keep = screen[0, t * (COLS // ABLK) + b].astype(F32)
            kept = raw[n, :, cols] * jnp.full((VIRT, ABLK), keep, F32).astype(BF16)
            to[:, cols] = kept
            if n == 3:
                also[o, :, cols] = kept
        if n == 0:
            pl.semaphore_wait(barrier, len(greet))
        if n < 4:
            key = list(near)[n]
            near_in[key] = send(slabs.at[n], rows.at[o, t % 2], sa.at[n], ra.at[n], near[key][0])
        elif n < 6:
            for p, span in enumerate(PARTS):
                k = (n - 4) * 2 + p
                far_in[n - 4, p] = send(
                    slabs.at[n, span], also.at[o, span], sr.at[k], rr.at[k], far[n - 4][0]
                )
    level_in = [
        send(levels.at[o], levels.at[o], se.at[n], re.at[n], d) for n, d in enumerate(everyone)
    ]
    to_partner = send(rows.at[o], rows.at[o], sa.at[4], ra.at[4], partner)
    also_in = send(slabs.at[0], also.at[o], sa.at[5], ra.at[5], partner)

    for half in (0, 1):
        vrow[half * 128 : (half + 1) * 128, :] = jnp.broadcast_to(
            energies[half : half + 1, :], (128, 128)
        ).T
    atom = lax.broadcasted_iota(jnp.int32, (3, 128), 1)
    for b in range(owner.shape[0]):
        spot = jnp.sum(jnp.where(atom == owner[b], positions[...], 0.0), axis=1, keepdims=True)
        where[0:3, b * ABLK : (b + 1) * ABLK] = jnp.broadcast_to(spot, (3, ABLK))
    pick = (
        lax.broadcasted_iota(jnp.int32, (CHUNK, 16 * CHUNK), 1) % CHUNK
        == lax.broadcasted_iota(jnp.int32, (CHUNK, 16 * CHUNK), 0)
    ).astype(F32).astype(BF16)

    def product(slot):
        r0, r1 = SLOTS[slot]
        first, second = (c + r0) % 4, (c + r1) % 4
        if slot in OPEN:
            first, second = jnp.minimum(first, second), jnp.maximum(first, second)
        lead = first * 2 + h
        for hc in (0, 1):
            s = dot_nt(rows[lead, 0], rows[second * 2 + hc, 0])
            s += dot_nt(rows[lead, 1], rows[second * 2 + hc, 1])
            part[slot, :, hc * VIRT : (hc + 1) * VIRT] = s.astype(BF16)

    def pass_on(n, came, src, span=slice(0, VIRT)):
        came.wait_recv()
        piece = rows.at[src, h, span]
        return send(piece, piece, sf.at[n], rf.at[n], partner)

    plane_wait = {}

    def share_products(g):
        lo, hi = GROUPS[g]
        for j, (d, qd) in plane_peers.items():
            there = pl.ds(pl.multiple_of(qd * CHUNK, CHUNK), CHUNK)
            plane_wait[g, j] = send(
                part.at[lo:hi, there, :], plane_in.at[lo:hi, j], sp.at[g, j], rp.at[g, j], d
            )

    mine = pl.ds(pl.multiple_of(q * CHUNK, CHUNK), CHUNK)

    def block_id(slot):
        r0, r1 = SLOTS[slot]
        if r0 == r1:
            return (c + r0) % 4
        if slot in OPEN:
            return 8 + (c + r0) % 2
        return 4 + (c + r0) % 4

    def sum_plane(g):
        lo, hi = GROUPS[g]
        for j in plane_peers:
            plane_wait[g, j].wait_recv()
        for slot in range(lo, hi):
            plane_in[slot, 0] = part[slot, mine, :]
            terms = plane_in[slot].reshape(16 * CHUNK, 2 * VIRT)
            s = dot_nn(pick, terms)
            plane_sum[block_id(slot)] = s
            plane_out[block_id(slot)] = s.astype(BF16)

    to_partner.wait_recv()
    product(0)
    share_products(0)
    passed = []
    for n, ((way, flip), came) in enumerate(near_in.items()):
        src = chip(-side if way == flip else side) * 2 + (h + flip) % 2
        passed.append(pass_on(n, came, src))
    for cp in passed:
        cp.wait_recv()
    for g in (1, 2):
        for slot in range(*GROUPS[g]):
            product(slot)
        share_products(g)
    through = {}
    for p, span in enumerate(PARTS):
        for flip in (0, 1):
            far_in[flip, p].wait_recv()
            src = chip(side) * 2 + (h + flip) % 2
            k = flip * 2 + p
            through[flip, p] = send(
                also.at[src, span], rows.at[src, other, span], st.at[k], rt.at[k], buddy
            )
    passed = []
    for (flip, p), came in through.items():
        src = chip(2) * 2 + (other + flip) % 2
        passed.append(pass_on(4 + flip * 2 + p, came, src, PARTS[p]))
    for cp in passed:
        cp.wait_recv()

    def lend(n, src):
        return send(
            rows.at[pl.ds(src * 2, 2), h], also.at[pl.ds(src * 2, 2)], sm.at[n], rm.at[n], buddy
        )

    mid = [lend(0, c)]
    for g in (3, 4):
        for slot in range(*GROUPS[g]):
            product(slot)
        share_products(g)
    for g in range(len(GROUPS)):
        sum_plane(g)

    def share_of(k):
        return (
            pl.ds((k // 4) * 5, 5),
            slice(None),
            pl.ds(pl.multiple_of((k % 4) * 128, 128), 128),
        )

    z_wait = {}
    for dz, (d, zd) in z_peers.items():
        z_wait[dz] = send(plane_out.at[share_of(zd)], z_in.at[dz], sz.at[dz], rz.at[dz], d)
    for dz in z_peers:
        z_wait[dz].wait_recv()

    for cp in level_in:
        cp.wait_recv()
    hc = (z % 4) // 2
    va = vrow[mine, :]
    vb = energies[pl.ds(z % 2, 1), :]
    lanes = pl.ds(pl.multiple_of((z % 4) * 128, 128), 128)
    for t in range(5):
        b = (z // 4) * 5 + t
        s = plane_sum[b, :, lanes]
        for dz in z_peers:
            s += z_in[dz, t].astype(F32)
        first = b % 4
        lead = first * 2 + h
        second = jnp.where(b < 4, first, jnp.where(b < 8, (first + 1) % 4, first + 2))
        ea = levels[lead].astype(F32)
        eb = levels[second * 2 + hc].astype(F32)
        z_amps[b, :, lanes] = (s / ((va - ea) + (vb - eb))).astype(BF16)
    y_wait = {}
    for dz, (d, _) in z_peers.items():
        y_wait[dz] = send(
            z_amps.at[share_of(z)], z_amps.at[share_of(z)], sy.at[dz], ry.at[dz], d
        )
    for dz in z_peers:
        y_wait[dz].wait_recv()
    mid.append(lend(1, chip(side)))

    here = pl.ds(pl.multiple_of(h * VIRT + q * CHUNK, CHUNK), CHUNK)
    for k, slot in enumerate(KEPT):
        amps[k, here, :] = z_amps[block_id(slot)]

    def piece(g, half, i, j):
        i, j = (i, j) if half == 0 else (j, i)
        src_q = ((x + 4 - i) % 4) * 4 + (y + 4 - j) % 4
        rows_ = pl.ds(pl.multiple_of(h * VIRT + src_q * CHUNK, CHUNK), CHUNK)
        return amps.at[slice(*SPREADS[g]), rows_, half * VIRT : (half + 1) * VIRT]

    def peer(half, i, j):
        i, j = (i, j) if half == 0 else (j, i)
        return plane_peers[i * 4 + j][0]

    g_wait, h_wait = {}, {0: [], 1: []}

    def spread(g, half, i):
        for j in (1, 3, 2):
            k = i * 4 + j
            g_wait[g, half, k] = send(
                piece(g, half, i, 0), piece(g, half, i, 0), sg.at[g, half, k], rg.at[g, half, k], peer(half, 0, j)
            )

    def to_other(g, n, rows_, cols):
        ref = amps.at[slice(*SPREADS[g]), rows_, cols]
        h_wait[g].append(send(ref, ref, sh.at[g, n], rh.at[g, n], partner))

    def begin(g):
        for i in (1, 3, 2):
            for half in (0, 1):
                k = i * 4
                ref = piece(g, half, 0, 0)
                g_wait[g, half, k] = send(ref, ref, sg.at[g, half, k], rg.at[g, half, k], peer(half, i, 0))
        for half in (0, 1):
            spread(g, half, 0)

    def relay(g):
        for i in (1, 3, 2):
            for half in (0, 1):
                g_wait[g, half, i * 4].wait_recv()
                spread(g, half, i)

    def collect(g):
        for i in (0, 1, 3, 2):
            for j in (1, 3, 2):
                g_wait[g, 0, i * 4 + j].wait_recv()
            first = pl.multiple_of(h * VIRT + ((x + 4 - i) % 4) * 4 * CHUNK, 4 * CHUNK)
            to_other(g, i, pl.ds(first, 4 * CHUNK), slice(0, VIRT))
        for i in (0, 1, 3, 2):
            for j in (1, 3, 2):
                g_wait[g, 1, i * 4 + j].wait_recv()
        own = pl.ds(pl.multiple_of(h * VIRT, VIRT), VIRT)
        to_other(g, 4, own, slice(VIRT, 2 * VIRT))
        for cp in h_wait[g]:
            cp.wait_recv()

    def lay(n, slot, as_is):
        @pl.when(as_is)
        def _():
            turned[n] = amps[slot]

        @pl.when(jnp.logical_not(as_is))
        def _():
            turned[n] = amps[slot].T

    def gamma_rows(factors, hr, target, weights):
        span = pl.ds(pl.multiple_of(hr * VIRT, VIRT), VIRT)
        row_chip, send_to = target
        ro = row_chip * 2 + hr
        for k in (0, 1):
            acc = None
            for dot, ref, co in factors:
                for hcol in range(2):
                    half = slice(hcol * VIRT, (hcol + 1) * VIRT)
                    block = ref[span, half] if dot is dot_nn else ref[half, span]
                    src = co * 2 + hcol
                    term = dot(block, rows[src, h] if k == 0 else also[src])
                    acc = term if acc is None else acc + term
            out = acc.astype(BF16)
            t = o if k == 0 else buddy_o
            cols = pl.ds(pl.multiple_of(t * COLS, COLS), COLS)
            if send_to is None:
                gamma[:, cols] = out
            else:
                n, d = send_to
                gout[n + k] = out
                ready.append((n + k, cols, d))
                if n == 0:
                    send_ready()
            m = rows[ro, h] if k == 0 else also[ro]
            weights[k] += jnp.sum(out.astype(F32) * m.astype(F32), axis=0, keepdims=True)

    def send_ready():
        for n, cols, d in ready:
            b_wait.append(send(gout.at[n], gamma.at[:, cols], sb.at[n], rb.at[n], d))
        ready.clear()

    ready = []

    b_wait = []
    weights = [jnp.zeros((1, COLS), F32), jnp.zeros((1, COLS), F32)]
    begin(0)
    relay(0)
    begin(1)
    relay(1)
    also_in.wait_recv()
    for cp in mid:
        cp.wait_recv()
    collect(0)
    lay(0, 2 + h, h == 1)
    lay(1, 5 + h, h == 0)
    lay(2, 4, chip(side) < 2)
    factors = (
        (dot_nn, turned.at[0], c),
        (dot_nn, amps.at[h], chip(side)),
        (dot_nn, turned.at[1], chip(2)),
        (dot_nn, turned.at[2], chip(-side)),
    )
    for flip in (0, 1):
        hr = (h + flip) % 2
        gamma_rows(factors, hr, (chip(side), (flip * 2, near[0, flip][0])), weights)
    later = [*ready]
    ready.clear()
    collect(1)
    lay(3, 8, c < 2)
    factors = (
        (dot_nn, amps.at[7], c),
        (dot_nn, amps.at[2], chip(1)),
        (dot_nn, turned.at[3], chip(2)),
        (dot_tn, amps.at[3], chip(3)),
    )
    gamma_rows(factors, other, (c, (4, partner)), weights)
    send_ready()
    gamma_rows(factors, h, (c, None), weights)

    for k in (0, 1):
        wmine[k * 8 : k * 8 + 8, :] = jnp.broadcast_to(weights[k], (8, COLS))
        wall[o, k * 8 : k * 8 + 8, :] = jnp.broadcast_to(weights[k], (8, COLS))
    w_wait = [
        send(wmine, wall.at[o], sw.at[n], rw.at[n], d) for n, d in enumerate(everyone)
    ]
    ready.extend(later)
    send_ready()
    for cp in w_wait:
        cp.wait_recv()
    for t in range(8):
        cols = slice(t * COLS, (t + 1) * COLS)
        pair = ((t // 2 + 2 * (t % 2) - 1) % 4) * 2 + 1 - t % 2
        w = wall[t, 0:1, :] + wall[pair, 8:9, :]
        for i in range(3):
            for j in range(3):
                n = 3 * i + j
                virial[n : n + 1, cols] = where[i : i + 1, cols] * where[j : j + 1, cols] * w
    for cp in b_wait:
        cp.wait_recv()
    for cp in sent:
        cp.wait_send()


def write_out(gamma_in, virial_in, gamma, virial, sem):
    copies = [
        pltpu.make_async_copy(gamma_in, gamma, sem.at[0]),
        pltpu.make_async_copy(virial_in, virial, sem.at[1]),
    ]
    for cp in copies:
        cp.start()
    for cp in copies:
        cp.wait()


def body(coeffs, occ_energy, virt_energy, screen, owner, positions):
    occ_dev, virt, aux_dev = coeffs.shape
    energies = jnp.concatenate(
        [virt_energy.reshape(2, 128), jnp.broadcast_to(occ_energy[:, None], (1, 128))]
    ).astype(F32)
    vmem = pl.BlockSpec(memory_space=pltpu.VMEM)
    smem = pl.BlockSpec(memory_space=pltpu.SMEM)
    dma = pltpu.SemaphoreType.DMA
    gamma, virial = pl.pallas_call(
        kernel,
        out_shape=(pltpu.VMEM((VIRT, aux_dev), BF16), pltpu.VMEM((9, aux_dev), F32)),
        in_specs=[smem, smem, pl.BlockSpec(memory_space=pltpu.HBM), vmem, vmem],
        out_specs=(vmem, vmem),
        scratch_shapes=[
            pltpu.VMEM((8, VIRT, COLS), BF16),
            pltpu.VMEM((6, VIRT, COLS), BF16),
            pltpu.VMEM((8, 2, VIRT, COLS), BF16),
            pltpu.VMEM((8, VIRT, COLS), BF16),
            pltpu.VMEM((8, TAIL, 128), BF16),
            pltpu.VMEM((VIRT, 128), F32),
            pltpu.VMEM((NBLK, VIRT, 2 * VIRT), BF16),
            pltpu.VMEM((NBLK, 16, CHUNK, 2 * VIRT), BF16),
            pltpu.VMEM((NBLK, CHUNK, 2 * VIRT), F32),
            pltpu.VMEM((NBLK, CHUNK, 2 * VIRT), BF16),
            pltpu.VMEM((8, 5, CHUNK, 128), BF16),
            pltpu.VMEM((NBLK, CHUNK, 2 * VIRT), BF16),
            pltpu.VMEM((NBLK - 1, 2 * VIRT, 2 * VIRT), BF16),
            pltpu.VMEM((4, 2 * VIRT, 2 * VIRT), BF16),
            pltpu.VMEM((6, VIRT, COLS), BF16),
            pltpu.VMEM((16, COLS), F32),
            pltpu.VMEM((8, 16, COLS), F32),
            pltpu.VMEM((8, aux_dev), F32),
            dma((7,)), dma((7,)), dma((8,)), dma((6,)), dma((6,)), dma((4,)), dma((4,)), dma((4,)), dma((4,)),
            dma((8,)), dma((8,)), dma((2,)), dma((2,)),
            dma((5, 16)), dma((5, 16)), dma((8,)), dma((8,)), dma((8,)), dma((8,)),
            dma((2, 2, 16)), dma((2, 2, 16)), dma((2, 5)), dma((2, 5)),
            dma((6,)), dma((6,)), dma((7,)), dma((7,)),
        ],
        compiler_params=pltpu.CompilerParams(
            collective_id=0, has_side_effects=True, vmem_limit_bytes=64684032
        ),
    )(screen, owner, coeffs.reshape(VIRT, aux_dev), energies, positions)
    gamma, virial = pl.pallas_call(
        write_out,
        out_shape=(
            jax.ShapeDtypeStruct((VIRT, aux_dev), BF16),
            jax.ShapeDtypeStruct((9, aux_dev), F32),
        ),
        in_specs=[pl.BlockSpec(memory_space=pl.ANY)] * 2,
        out_specs=(pl.BlockSpec(memory_space=pl.ANY),) * 2,
        scratch_shapes=[dma((2,))],
        compiler_params=pltpu.CompilerParams(vmem_limit_bytes=1024 * 1024),
    )(gamma, virial)
    return gamma.reshape(occ_dev, virt, aux_dev), virial


def solution(mesh):
    placed = (P("occ", None, "aux"), P("occ"), P(), P("occ", "aux"), P("aux"), P())
    return jax.shard_map(
        body,
        mesh=mesh,
        in_specs=placed,
        out_specs=(P("occ", None, "aux"), P(None, "aux")),
        check_vma=False,
    )
```
